32 devices in a mesh: exp: 4 (over y, x), imp: 2 (over core), wk: 4 (over z).
Axes of the slice: x: 2, y: 2, z: 4, core: 2. Of those that a mesh axis runs over, the one named last changes fastest.
Arguments:
- flows: float32 [4, 2048, 256], P('wk', 'exp', 'imp'), may hold values from 0.0112 to 284, as said below
- importer_factor: float32 [256, 256], P('imp'), may hold values from -0.5 to 1.5
- week_factor: float32 [4, 256], P('wk'), may hold values from 0 to 1
Outputs:
- exporter_out: float32 [2048, 256], P('exp')
- importer_out: float32 [256, 256], P('imp')
- week_out: float32 [4, 256], P('wk')
The draws below stay inside these ranges and needn't reach their ends.
Inputs may be any that keep to these rules, and one draw needn't show every extreme that they name: `flows`: flows are positive.
All inputs are finite; a program needn't handle non-finite values.
Results may differ from the reference program's by a relative error of at most 0.00022.
Values sent between devices are 32-bit elements; how exact they have to be, the bound alone decides.
No kernel may reach another device: no remote copies, remote signals or barrier semaphores. Data moves between devices by JAX's collectives and lax.ppermute only.
A program may use at most 64 MiB of HBM per device.

```python
import math
import jax
import jax.numpy as jnp
from jax import lax

R = 256
I = 2048
J = 256
K = 4


def draw_flows(key, part):
    keys = jax.random.split(key, 4)
    lo = math.log(0.3)
    hi = math.log(3.0)
    rise = math.log(3.0)
    rows = jnp.exp(jax.random.uniform(keys[0], (I,), jnp.float32, lo, hi) + rise * jnp.arange(I, dtype=jnp.float32) / I)
    cols = jnp.exp(jax.random.uniform(keys[1], (J,), jnp.float32, lo, hi) + rise * jnp.arange(J, dtype=jnp.float32) / J)
    weeks = jnp.exp(jax.random.uniform(keys[2], (K,), jnp.float32, math.log(0.5), math.log(2.0)))
    noise = jax.random.uniform(keys[3], (K, I, J), jnp.float32, 0.25, 1.75)
    return weeks[:, None, None] * rows[None, :, None] * cols[None, None, :] * noise


def block_scale(stream_key, extent, cuts, low, top_value):
    loudness, own = 1.0, jax.random.fold_in(stream_key, 6)
    for position, blocks in cuts:
        draws = jnp.exp(jax.random.uniform(jax.random.fold_in(own, position), (blocks,), jnp.float32, low / len(cuts), top_value / len(cuts)))
        loudness = loudness * jnp.repeat(draws, extent[position] // blocks).reshape([-1 if axis == position else 1 for axis in range(len(extent))])
    return loudness


def setup_inputs(seed: int = 0) -> dict:
    arg_keys = jax.random.split(jax.random.key(seed), 4)
    flows = draw_flows(jax.random.fold_in(arg_keys[3], 71), 0)
    importer_factor = jnp.clip(-0.5 + 2.0 * jax.random.uniform(arg_keys[1], (J, R), jnp.float32) ** block_scale(arg_keys[1], (J, R), ((0, 2),), -0.2, 0.2), -0.5, 1.5)
    week_factor = jnp.clip(1.0 * jax.random.uniform(arg_keys[2], (K, R), jnp.float32) ** block_scale(arg_keys[2], (K, R), ((0, 4),), -0.2, 0.2), 0.0, 1.0)
    return {"flows": flows, "importer_factor": importer_factor, "week_factor": week_factor}


ridge = 0.2
eps = 1e-06
hp = lax.Precision.HIGHEST

def solve_rows(m, g1, g2):
    h = g1 * g2
    lam = ridge * jnp.trace(h) / h.shape[0]
    v = h + lam * jnp.eye(h.shape[0], dtype=jnp.float32)
    chol = jnp.linalg.cholesky(v)
    return jax.scipy.linalg.cho_solve((chol, True), m.T).T

def unit_cols(x):
    scale = jnp.sqrt(lax.optimization_barrier(jnp.sum(x * x, 0)) / x.shape[0] + eps)
    y = x / scale
    return (y, jnp.dot(y.T.astype(jnp.float32), y.astype(jnp.float32), precision=hp, preferred_element_type=jnp.float32))

def reference(flows, importer_factor, week_factor):
    row_tot = lax.optimization_barrier(jnp.sum(flows, 2))
    col_tot = lax.optimization_barrier(jnp.sum(flows, 1))
    grand = lax.optimization_barrier(jnp.sum(row_tot, 1))
    resid = flows - row_tot[:, :, None] * col_tot[:, None, :] / grand[:, None, None]
    gram_b = jnp.dot(importer_factor.T.astype(jnp.float32), importer_factor.astype(jnp.float32), precision=hp, preferred_element_type=jnp.float32)
    gram_c = jnp.dot(week_factor.T.astype(jnp.float32), week_factor.astype(jnp.float32), precision=hp, preferred_element_type=jnp.float32)
    inner = jnp.einsum('kij,jr->kir', resid, importer_factor, precision=hp)
    m_a = lax.optimization_barrier(jnp.sum(inner * week_factor[:, None, :], 0))
    fac_a, gram_a = unit_cols(solve_rows(m_a, gram_b, gram_c))
    weighted = fac_a[None, :, :] * week_factor[:, None, :]
    m_b = jnp.einsum('kij,kir->jr', resid, weighted, precision=hp)
    fac_b, gram_b2 = unit_cols(solve_rows(m_b, gram_a, gram_c))
    inner = jnp.einsum('kij,jr->kir', resid, fac_b, precision=hp)
    m_c = lax.optimization_barrier(jnp.sum(inner * fac_a[None, :, :], 1))
    fac_c, unused = unit_cols(solve_rows(m_c, gram_a, gram_b2))
    return (fac_a, fac_b, fac_c)
```

```python
import jax
import jax.numpy as jnp
from jax import lax
from jax.experimental import pallas as pl
from jax.experimental.pallas import tpu as pltpu
from jax.sharding import PartitionSpec as P

ridge = 0.2
eps = 1e-06
hp = lax.Precision.HIGHEST
block = 32


def dot(a, b):
    return jnp.dot(a, b, precision=hp, preferred_element_type=jnp.float32)


def pivot_panel(panel):
    groups, tiles = len(panel), len(panel[0])
    lane = lax.broadcasted_iota(jnp.int32, (8, 128), 1)
    sub = lax.broadcasted_iota(jnp.int32, (8, 128), 0)
    part = [list(r) for r in panel]
    for g in range(groups):
        cols = [
            [jnp.broadcast_to(part[h][0][:, 8 * g + q : 8 * g + q + 1], (8, 128)) for h in range(groups)]
            for q in range(8)
        ]
        for q in range(8):
            col = cols[q]
            inv = 1.0 / jnp.broadcast_to(col[g][q : q + 1, :], (8, 128))
            here = lane == 8 * g + q
            this = sub == q
            rows = []
            for t in range(tiles):
                row = jnp.broadcast_to(part[g][t][q : q + 1, :], (8, 128))
                if t == 0:
                    row = jnp.where(here, 1.0, row)
                rows.append(row * inv)
            for h in range(groups):
                for t in range(tiles):
                    base = jnp.where(here, 0.0, part[h][t]) if t == 0 else part[h][t]
                    new = base - col[h] * rows[t]
                    part[h][t] = jnp.where(this, rows[t], new) if h == g else new
            for q2 in range(q + 1, 8):
                factor = jnp.broadcast_to(cols[q2][g][q : q + 1, :], (8, 128)) * inv
                for h in range(groups):
                    new = cols[q2][h] - col[h] * factor
                    cols[q2][h] = jnp.where(this, factor, new) if h == g else new
    return jnp.concatenate([jnp.concatenate(r, axis=1) for r in part], axis=0)


def inverse_kernel(v_ref, o_ref, a_ref):
    n = v_ref.shape[0]
    a_ref[...] = v_ref[...]

    def step(_, carry):
        panel = [
            [a_ref[8 * g : 8 * g + 8, 128 * t : 128 * t + 128] for t in range(n // 128)]
            for g in range(block // 8)
        ]
        top = pivot_panel(panel)
        rest = a_ref[block:, :]
        lane = lax.broadcasted_iota(jnp.int32, rest.shape, 1)
        new = jnp.where(lane < block, 0.0, rest) - dot(rest[:, :block], top)
        a_ref[: n - block, :] = pltpu.roll(new, n - block, 1)
        a_ref[n - block :, :] = pltpu.roll(top, n - block, 1)
        return carry

    lax.fori_loop(0, n // block, step, 0)
    o_ref[...] = a_ref[...]


def inverse(v):
    n = v.shape[0]
    return pl.pallas_call(
        inverse_kernel,
        out_shape=jax.ShapeDtypeStruct((n, n), jnp.float32),
        in_specs=[pl.BlockSpec(memory_space=pltpu.VMEM)],
        out_specs=pl.BlockSpec(memory_space=pltpu.VMEM),
        scratch_shapes=[pltpu.VMEM((n, n), jnp.float32)],
        name="inverse",
    )(v)


def ridge_inverse(g1, g2):
    h = g1 * g2
    n = h.shape[0]
    eye = jnp.eye(n, dtype=jnp.float32)
    return inverse(h + (ridge * jnp.trace(h) / n) * eye)


def swap(x, axis, bit):
    n = lax.axis_size(axis)
    return lax.ppermute(x, axis, [(i, i ^ bit) for i in range(n)])


def bits(axis):
    n = lax.axis_size(axis)
    return [1 << b for b in range(n.bit_length() - 1)]


def total(x, axis):
    for bit in bits(axis):
        x = x + swap(x, axis, bit)
    return x


def scatter_total(x, axis):
    me = lax.axis_index(axis)
    for bit in reversed(bits(axis)):
        half = x.reshape((2, x.shape[0] // 2) + x.shape[1:])
        mine = jnp.where((me & bit) != 0, 1, 0)
        keep = lax.dynamic_index_in_dim(half, mine, 0, keepdims=False)
        give = lax.dynamic_index_in_dim(half, 1 - mine, 0, keepdims=False)
        x = keep + swap(give, axis, bit)
    return x


def gather_rows(x, axis):
    me = lax.axis_index(axis)
    for bit in bits(axis):
        other = swap(x, axis, bit)
        mine = (me & bit) != 0
        x = jnp.concatenate([jnp.where(mine, other, x), jnp.where(mine, x, other)], axis=0)
    return x


def by_index(pieces, axis):
    me = lax.axis_index(axis)
    out = jnp.zeros((len(pieces),) + pieces[0].shape, jnp.float32)
    for d, piece in enumerate(pieces):
        out = lax.dynamic_update_slice(out, piece[None], ((me ^ d),) + (0,) * piece.ndim)
    return out


def scale_of(gram, count):
    n = gram.shape[0]
    diag = jnp.where(jnp.eye(n, dtype=jnp.bool_), gram, 0.0)
    one = jnp.sqrt(jnp.sum(diag, 0) / count + eps)
    two = jnp.sqrt(jnp.sum(diag, 1) / count + eps)
    return one, gram / (two[:, None] * one[None, :])


def per_device(flows, importer_factor, week_factor):
    f = flows[0]
    w = week_factor
    rank = w.shape[1]
    rows_here, cols_here = f.shape
    weeks = lax.axis_size("wk")
    me_k = lax.axis_index("wk")
    me_i = lax.axis_index("imp")
    ni = lax.axis_size("imp")

    row_part = jnp.sum(f, 1)
    col_part = jnp.sum(f, 0)
    small = jnp.concatenate([dot(col_part[None], importer_factor)[0], jnp.sum(col_part)[None], col_part])
    m_part = dot(f, importer_factor * w)
    gram_b = total(dot(importer_factor.T, importer_factor), "imp")
    row_tot = total(row_part, "imp")
    share = scatter_total(m_part, "imp")

    pad = -rows_here % rank
    extra = jnp.concatenate([w, jnp.pad(row_tot, (0, pad)).reshape(-1, rank)], axis=0)
    chunk = share.shape[0] // weeks
    cut = share.reshape(weeks, chunk, rank)
    got = []
    for d in range(weeks):
        give = jnp.concatenate([lax.dynamic_index_in_dim(cut, me_k ^ d, 0, keepdims=False), extra], axis=0)
        got.append(swap(give, "wk", d) if d else give)
    own = sum(g[:chunk] for g in got[1:]) + got[0][:chunk]
    tails = by_index([g[chunk:] for g in got], "wk")
    w_all = tails[:, 0]
    row_all = tails[:, 1:].reshape(weeks, -1)[:, :rows_here]

    gram_c = dot(w_all.T, w_all)
    inv_a = ridge_inverse(gram_b, gram_c)

    small = total(small, "exp")
    heads = total(small[: rank + 1], "imp")
    grand = heads[rank]
    shift = w * (heads[:rank] / grand)[None]
    col_mean = small[rank + 1 :] / grand

    give = jnp.concatenate([own, shift], axis=0)
    got = by_index([swap(give, "wk", d) if d else give for d in range(weeks)], "wk")
    shifts = got[:, chunk]
    m_rows = gather_rows(got[:, :chunk].reshape(-1, rank), "imp")
    m_a = m_rows - dot(row_all.T, shifts)
    raw_a = dot(m_a, inv_a)

    resid = f - row_tot[:, None] * col_mean[None, :]
    t_part = dot(resid.T, raw_a)
    mine = lax.dynamic_slice(raw_a, (0, me_i * (rank // ni)), (rows_here, rank // ni))
    g_part = dot(mine.T, raw_a)
    g_a = gather_rows(total(g_part, "exp"), "imp")
    scale_a, gram_a = scale_of(g_a, rows_here * lax.axis_size("exp"))
    fac_a = raw_a / scale_a
    inv_b = ridge_inverse(gram_a, gram_c)

    t = total(t_part, "exp") / scale_a
    m_b = total(t * w, "wk")
    raw_b = dot(m_b, inv_b)
    g_b = total(dot(raw_b.T, raw_b), "imp")
    scale_b, gram_b2 = scale_of(g_b, cols_here * ni)
    fac_b = raw_b / scale_b
    inv_c = ridge_inverse(gram_a, gram_b2)

    m_mine = total(jnp.sum(fac_b * t, 0)[None], "imp")
    m_c = by_index([swap(m_mine, "wk", d) if d else m_mine for d in range(weeks)], "wk")[:, 0]
    raw_c = dot(m_c, inv_c)
    scale_c = jnp.sqrt(jnp.sum(raw_c * raw_c, 0) / weeks + eps)
    fac_c = lax.dynamic_slice(raw_c, (me_k, 0), (1, rank)) / scale_c
    return (fac_a, fac_b, fac_c)


def solution(mesh):
    in_specs = (P("wk", "exp", "imp"), P("imp", None), P("wk", None))
    out_specs = (P("exp", None), P("imp", None), P("wk", None))
    return jax.shard_map(
        per_device, mesh=mesh, in_specs=in_specs, out_specs=out_specs, check_vma=False
    )
```

```python
import jax
import jax.numpy as jnp
from jax import lax
from jax.experimental import pallas as pl
from jax.experimental.pallas import tpu as pltpu
from jax.sharding import PartitionSpec as P


ridge = 0.2
eps = 1e-06
hp = lax.Precision.HIGHEST
block = 32


def dot(a, b):
    return jnp.dot(a, b, precision=hp, preferred_element_type=jnp.float32)


def pivot_panel(panel):
    groups, tiles = len(panel), len(panel[0])
    lane = lax.broadcasted_iota(jnp.int32, (8, 128), 1)
    sub = lax.broadcasted_iota(jnp.int32, (8, 128), 0)
    part = [list(r) for r in panel]
    for g in range(groups):
        cols = [
            [jnp.broadcast_to(part[h][0][:, 8 * g + q : 8 * g + q + 1], (8, 128)) for h in range(groups)]
            for q in range(8)
        ]
        for q in range(8):
            col = cols[q]
            inv = 1.0 / jnp.broadcast_to(col[g][q : q + 1, :], (8, 128))
            here = lane == 8 * g + q
            this = sub == q
            rows = []
            for t in range(tiles):
                row = jnp.broadcast_to(part[g][t][q : q + 1, :], (8, 128))
                if t == 0:
                    row = jnp.where(here, 1.0, row)
                rows.append(row * inv)
            for h in range(groups):
                for t in range(tiles):
                    base = jnp.where(here, 0.0, part[h][t]) if t == 0 else part[h][t]
                    new = base - col[h] * rows[t]
                    part[h][t] = jnp.where(this, rows[t], new) if h == g else new
            for q2 in range(q + 1, 8):
                factor = jnp.broadcast_to(cols[q2][g][q : q + 1, :], (8, 128)) * inv
                for h in range(groups):
                    new = cols[q2][h] - col[h] * factor
                    cols[q2][h] = jnp.where(this, factor, new) if h == g else new
    return jnp.concatenate([jnp.concatenate(r, axis=1) for r in part], axis=0)


def eliminate(a_ref, count):
    n = a_ref.shape[0]

    def step(_, carry):
        panel = [
            [a_ref[8 * g : 8 * g + 8, 128 * t : 128 * t + 128] for t in range(n // 128)]
            for g in range(block // 8)
        ]
        top = pivot_panel(panel)
        rest = a_ref[block:, :]
        lane = lax.broadcasted_iota(jnp.int32, rest.shape, 1)
        new = jnp.where(lane < block, 0.0, rest) - dot(rest[:, :block], top)
        a_ref[: n - block, :] = pltpu.roll(new, n - block, 1)
        a_ref[n - block :, :] = pltpu.roll(top, n - block, 1)
        return carry

    lax.fori_loop(0, count, step, 0)


def near(x):
    return pltpu.with_memory_space_constraint(x, pltpu.VMEM)


def call(kernel, outs, *args, smem=0, scratch=()):
    specs = [pl.BlockSpec(memory_space=pltpu.SMEM)] * smem
    specs += [pl.BlockSpec(memory_space=pltpu.VMEM)] * (len(args) - smem)
    many = isinstance(outs, list)
    shapes = [pltpu.VMEM(s, jnp.float32) for s in (outs if many else [outs])]
    vmem = [pl.BlockSpec(memory_space=pltpu.VMEM)] * len(shapes)
    return pl.pallas_call(
        kernel,
        out_shape=shapes if many else shapes[0],
        in_specs=specs,
        out_specs=vmem if many else vmem[0],
        scratch_shapes=scratch,
    )(*args[:smem], *[near(a) for a in args[smem:]])


def inverse_piece(state, count):
    def kernel(v_ref, o_ref):
        o_ref[...] = v_ref[...]
        eliminate(o_ref, count)

    return call(kernel, state.shape, state)


def inverse_and_unit(state, count, raw, scale):
    def kernel(v_ref, raw_ref, scale_ref, o_ref, unit_ref, buf, sem):
        buf[...] = raw_ref[...] / scale_ref[...]
        copy = pltpu.make_async_copy(buf, unit_ref, sem)
        copy.start()
        o_ref[...] = v_ref[...]
        eliminate(o_ref, count)
        copy.wait()

    vmem = pl.BlockSpec(memory_space=pltpu.VMEM)
    return pl.pallas_call(
        kernel,
        out_shape=[pltpu.VMEM(state.shape, jnp.float32), jax.ShapeDtypeStruct(raw.shape, jnp.float32)],
        in_specs=[vmem] * 3,
        out_specs=[vmem, pl.BlockSpec(memory_space=pl.ANY)],
        scratch_shapes=[pltpu.VMEM(raw.shape, jnp.float32), pltpu.SemaphoreType.DMA(())],
        name="inverse_unit",
    )(near(state), near(raw), near(scale))


def eye(n):
    return lax.broadcasted_iota(jnp.int32, (n, n), 0) == lax.broadcasted_iota(jnp.int32, (n, n), 1)


def outer(a, b):
    return lax.dot_general(a, b, (((0,), (0,)), ((), ())), precision=hp, preferred_element_type=jnp.float32)


def ridged(h):
    n = h.shape[0]
    on = eye(n)
    diag = jnp.where(on, h, 0.0)
    trace = jnp.sum(jnp.sum(diag, axis=0, keepdims=True), axis=1, keepdims=True)
    return h + jnp.where(on, trace * (ridge / n), 0.0)


def normalised(gram, count):
    diag = jnp.where(eye(gram.shape[0]), gram, 0.0)
    one = jnp.sqrt(jnp.sum(diag, axis=0, keepdims=True) / count + eps)
    two = jnp.sqrt(jnp.sum(diag, axis=1, keepdims=True) / count + eps)
    return one, gram * (1.0 / two) * (1.0 / one)


def after(x, *deps):
    return lax.optimization_barrier((x,) + deps)[0]


def swap(x, axis, bit):
    n = lax.axis_size(axis)
    return lax.ppermute(x, axis, [(i, i ^ bit) for i in range(n)])


def bits(axis):
    n = lax.axis_size(axis)
    return [1 << b for b in range(n.bit_length() - 1)]


def total(x, axis, some=None):
    for bit in bits(axis) if some is None else some:
        x = x + swap(x, axis, bit)
    return x


def total_crossed(x, axis, side):
    n, m = lax.axis_size(axis), lax.axis_size(side)
    order = bits(axis)
    for one, two in zip(order, reversed(order)):
        pairs = [(i * m + j, (i ^ (two if j & 1 else one)) * m + j) for i in range(n) for j in range(m)]
        x = x + lax.ppermute(x, (axis, side), pairs)
    return x


def gather_rows(x, axis):
    me = lax.axis_index(axis)
    for bit in bits(axis):
        other = swap(x, axis, bit)
        mine = (me & bit) != 0
        x = jnp.concatenate([jnp.where(mine, other, x), jnp.where(mine, x, other)], axis=0)
    return x


def open_kernel(pick_ref, f_ref, b_ref, w_ref, give_ref, row_ref, f_out_ref, b_out_ref, w_out_ref):
    f = f_ref[...]
    half = f.shape[0] // 2
    at = pl.multiple_of(pick_ref[0] * half, half)
    give_ref[:half, :] = dot(f_ref[pl.ds(at, half), :], b_ref[...] * w_ref[...])
    row = lax.dot_general(
        jnp.ones((8, f.shape[1]), jnp.float32), f, (((1,), (1,)), ((), ())), precision=hp, preferred_element_type=jnp.float32
    )[:1]
    row_ref[...] = row
    rank = give_ref.shape[1]
    give_ref[half:, :] = jnp.zeros_like(give_ref[half:, :])
    for n in range(f.shape[0] // rank):
        give_ref[half + n : half + n + 1, :] = row[:, n * rank : (n + 1) * rank]
    f_out_ref[...] = f
    b_out_ref[...] = b_ref[...]
    w_out_ref[...] = w_ref[...]


def rest_kernel(pick_ref, f_ref, b_ref, w_ref, keep_ref, small_ref, gram_ref):
    b = b_ref[...]
    half, cols = f_ref.shape[0] // 2, f_ref.shape[1]
    at = pl.multiple_of(pick_ref[0] * half, half)
    keep_ref[...] = dot(f_ref[pl.ds(at, half), :], b * w_ref[...])
    col = jnp.sum(f_ref[...], axis=0, keepdims=True)
    small_ref[...] = jnp.zeros_like(small_ref)
    small_ref[0:1, :] = dot(jnp.broadcast_to(col, (8, cols)), b)[:1]
    small_ref[1:2, :cols] = col
    small_ref[2:3, :] = jnp.broadcast_to(jnp.sum(col, axis=1, keepdims=True), (1, small_ref.shape[1]))
    gram_ref[...] = outer(b, b)


def cut_kernel(me_ref, own_ref, got_ref, row_ref, w_ref, *gives):
    half, rank = own_ref.shape
    chunk = half // len(gives)
    row = row_ref[...] + jnp.concatenate(
        [got_ref[half + n : half + n + 1, :] for n in range(row_ref.shape[1] // rank)], axis=1
    )
    for d, give in enumerate(gives):
        at = pl.multiple_of((me_ref[0] ^ d) * chunk, chunk)
        give[:chunk, :] = own_ref[pl.ds(at, chunk), :] + got_ref[pl.ds(at, chunk), :]
        give[chunk:, :] = jnp.zeros_like(give[chunk:, :])
        give[chunk : chunk + 1, :] = w_ref[...]
        for n in range(row_ref.shape[1] // rank):
            give[chunk + 1 + n : chunk + 2 + n, :] = row[:, n * rank : (n + 1) * rank]


def fold_kernel(*refs):
    *parts, heads_ref, small_ref, w_ref, give_ref, col_ref = refs
    chunk = give_ref.shape[0] - 8
    acc = parts[0][:chunk, :]
    for part in parts[1:]:
        acc = acc + part[:chunk, :]
    give_ref[:chunk, :] = acc
    grand = heads_ref[2:3, :]
    give_ref[chunk:, :] = jnp.zeros_like(give_ref[chunk:, :])
    give_ref[chunk : chunk + 1, :] = w_ref[...] * (heads_ref[0:1, :] / grand)
    cols = col_ref.shape[1]
    col_ref[...] = small_ref[1:2, :cols] / grand[:, :cols]


def first_kernel(me_ref, own_ref, other_ref, *refs):
    *parts, v_ref, gram_ref, row_ref, w_ref = refs
    rank = w_ref.shape[1]
    w_ref[...] = jnp.zeros_like(w_ref)
    row_ref[...] = jnp.zeros_like(row_ref)
    for d, part in enumerate(parts):
        chunk = part.shape[0] - 8
        at = me_ref[0] ^ d
        w_ref[pl.ds(at, 1), :] = part[chunk : chunk + 1, :]
        for n in range(row_ref.shape[1] // rank):
            row_ref[pl.ds(at, 1), n * rank : (n + 1) * rank] = part[chunk + 1 + n : chunk + 2 + n, :]
    gram = outer(w_ref[...], w_ref[...])
    gram_ref[...] = gram
    v_ref[...] = ridged((own_ref[...] + other_ref[...]) * gram)


def rows_kernel(me_ref, *refs):
    *parts, m_ref, shift_ref = refs
    shift_ref[...] = jnp.zeros_like(shift_ref)
    for d, part in enumerate(parts):
        chunk = part.shape[0] - 8
        at = me_ref[0] ^ d
        m_ref[pl.ds(pl.multiple_of(at * chunk, chunk), chunk), :] = part[:chunk, :]
        shift_ref[pl.ds(at, 1), :] = part[chunk : chunk + 1, :]


def exporter_kernel(
    me_ref, top_ref, own_ref, other_ref, row_all_ref, shift_ref, inv_ref, f_ref, col_ref, raw_ref, both_ref, m_ref, s_ref
):
    half = own_ref.shape[0]
    m_ref[pl.ds(pl.multiple_of(top_ref[0] * half, half), half), :] = own_ref[...]
    m_ref[pl.ds(pl.multiple_of((1 - top_ref[0]) * half, half), half), :] = other_ref[...]
    rank, cols = shift_ref.shape[1], f_ref.shape[1]
    s_ref[:, :rank] = shift_ref[...]
    week = lax.broadcasted_iota(jnp.int32, (s_ref.shape[0], cols), 0)
    s_ref[:, rank:] = jnp.where(week == me_ref[0], col_ref[...], 0.0)
    terms = outer(row_all_ref[...], s_ref[...])
    raw = dot(m_ref[...] - terms[:, :rank], inv_ref[...])
    raw_ref[...] = raw
    grams = both_ref.shape[0] - cols
    at = pl.multiple_of(top_ref[0] * grams, grams) if grams < rank else 0
    left = jnp.concatenate([raw_ref[:, pl.ds(at, grams)], f_ref[...] - terms[:, rank:]], axis=1)
    both_ref[...] = outer(left, raw)


def second_kernel(count, steps, g_ref, gram_c_ref, v_ref, gram_ref, scale_ref):
    scale, gram = normalised(g_ref[...], count)
    scale_ref[...] = scale
    gram_ref[...] = gram
    v_ref[...] = ridged(gram * gram_c_ref[...])
    eliminate(v_ref, steps)


def importer_kernel(own_ref, other_ref, scale_ref, inv_ref, t_ref, raw_ref, both_ref):
    raw = dot((own_ref[...] + other_ref[...]) / scale_ref[...], inv_ref[...])
    raw_ref[...] = raw
    rank = raw.shape[1]
    both_ref[:rank, :] = outer(raw, raw)
    both_ref[rank:, :] = jnp.zeros_like(both_ref[rank:, :])
    both_ref[rank : rank + 1, :] = jnp.sum(raw * t_ref[...], axis=0, keepdims=True)


def third_kernel(count, own_ref, other_ref, gram_a_ref, v_ref, scale_ref):
    rank = own_ref.shape[1]
    scale, gram = normalised(own_ref[:rank, :] + other_ref[:rank, :], count)
    scale_ref[...] = scale
    v_ref[...] = ridged(gram * gram_a_ref[...])


def week_kernel(*refs):
    *parts, scale_a_ref, scale_b_ref, inv_ref, o_ref, s_ref = refs
    s_ref[...] = jnp.zeros_like(s_ref)
    for i, part in enumerate(parts):
        s_ref[i : i + 1, :] = part[...] / scale_a_ref[...] / scale_b_ref[...]
    raw = dot(s_ref[...], inv_ref[...])
    scale = jnp.sqrt(jnp.sum(raw * raw, axis=0, keepdims=True) / len(parts) + eps)
    o_ref[...] = raw[:1] / scale


def shares(f, b, w, top, ni):
    rows, rank = f.shape[0], w.shape[1]
    if ni == 2 and rows % rank == 0 and rows // rank <= 7:
        give, row, f, b, w = pl.pallas_call(
            open_kernel,
            out_shape=[
                pltpu.VMEM(s, jnp.float32) for s in ((rows // 2 + 8, rank), (1, rows), f.shape, b.shape, w.shape)
            ],
            in_specs=[pl.BlockSpec(memory_space=pltpu.SMEM)] + [pl.BlockSpec(memory_space=pltpu.VMEM)] * 3,
            out_specs=[pl.BlockSpec(memory_space=pltpu.VMEM)] * 5,
            name="open",
        )(1 - top, f, b, w)
        got = swap(give, "imp", 1)
        keep, small, gram = call(rest_kernel, [(rows // 2, rank), (8, rank), (rank, rank)], top, f, b, w, smem=1)
        other = swap(gram, "imp", 1)
        return f, w, keep, got, row, small, gram, other
    low = bits("imp")[:-1]
    sums = jnp.sum(f, 1)[None]
    part = jnp.concatenate([dot(f, b * w).reshape(2, rows // 2, rank), jnp.zeros((2, 8, rank))], axis=1)
    part = total(part.at[:, rows // 2 : rows // 2 + rows // rank].set(sums.reshape(-1, rank)), "imp", low)
    keep = lax.dynamic_index_in_dim(part, top[0], 0, keepdims=False)[: rows // 2]
    got = swap(lax.dynamic_index_in_dim(part, 1 - top[0], 0, keepdims=False), "imp", ni // 2)
    row = part[0, rows // 2 : rows // 2 + rows // rank].reshape(1, rows)
    col = jnp.sum(f, 0)[None]
    wide = jnp.pad(col, ((0, 0), (0, rank - col.shape[1])))
    small = jnp.concatenate([dot(col, b), wide, jnp.full((1, rank), jnp.sum(col)), jnp.zeros((5, rank))], axis=0)
    gram = total(dot(b.T, b), "imp", low)
    return f, w, keep, got, row, small, gram, swap(gram, "imp", ni // 2)


def per_device(flows, importer_factor, week_factor):
    f = flows[0]
    w = week_factor
    rank = w.shape[1]
    rows, cols = f.shape
    weeks, ni, ne = lax.axis_size("wk"), lax.axis_size("imp"), lax.axis_size("exp")
    me_k = lax.axis_index("wk").astype(jnp.int32)[None]
    top = jnp.where((lax.axis_index("imp") & (ni // 2)) != 0, 1, 0).astype(jnp.int32)[None]
    steps = rank // block

    f, w, keep, got, row, small, gram_own, gram_other = shares(f, importer_factor, w, top, ni)
    small = small + swap(small, "exp", 1)

    chunk = keep.shape[0] // weeks
    gives = call(cut_kernel, [(chunk + 8, rank)] * weeks, me_k, keep, got, row, w, smem=1)
    got = [swap(g, "wk", d) if d else g for d, g in enumerate(gives)]
    for bit in bits("exp")[1:]:
        small = small + swap(small, "exp", bit)
    heads = total(small, "imp")
    give, col_mean = call(fold_kernel, [(chunk + 8, rank), (1, cols)], *got, heads, small, w)
    gathered = [swap(give, "wk", d) if d else give for d in range(weeks)]

    state, gram_c, row_all = call(
        first_kernel,
        [(rank, rank), (rank, rank), (-(-weeks // 8) * 8, rows)],
        me_k, after(gram_own, give), gram_other, *got,
        smem=1, scratch=[pltpu.VMEM((-(-weeks // 8) * 8, rank), jnp.float32)],
    )
    state = inverse_piece(state, steps // 2)
    *gathered, state = lax.optimization_barrier((*gathered, state))
    m_rows, shifts = call(rows_kernel, [(chunk * weeks, rank), (-(-weeks // 8) * 8, rank)], me_k, *gathered, smem=1)
    m_other = swap(m_rows, "imp", ni // 2)
    inv_a = inverse_piece(state, steps - steps // 2)

    grams = rank // 2 if ni == 2 and rank % 256 == 0 else rank
    raw_a, both = call(
        exporter_kernel,
        [(rows, rank), (grams + cols, rank)],
        me_k, top, m_rows, m_other, row_all, shifts, inv_a, f, col_mean,
        smem=2, scratch=[pltpu.VMEM((rows, rank), jnp.float32), pltpu.VMEM((-(-weeks // 8) * 8, rank + cols), jnp.float32)],
    )
    both = total_crossed(both, "exp", "imp")
    t = both[grams:]
    g_a = gather_rows(both[:grams], "imp") if grams < rank else both[:grams]

    def second(*refs):
        second_kernel(rows * ne, steps // 4, *refs)

    m_own = t * w
    m_got = swap(m_own, "wk", 1)
    state, gram_a, scale_a = call(second, [(rank, rank), (rank, rank), (1, rank)], g_a, gram_c)
    for bit in bits("wk")[1:]:
        state = inverse_piece(state, steps // 4)
        m_got, state = lax.optimization_barrier((m_got, state))
        m_own = m_own + m_got
        m_got = swap(m_own, "wk", bit)
    inv_b, fac_a = inverse_and_unit(after(state, m_own), steps - steps // 4 * len(bits("wk")), raw_a, scale_a)
    raw_b, both = call(importer_kernel, [(cols, rank), (rank + 8, rank)], m_own, m_got, scale_a, inv_b, t)
    for bit in bits("imp")[:-1]:
        both = both + swap(both, "imp", bit)
    got = swap(both, "imp", ni // 2)
    m_mine = both[rank : rank + 1] + got[rank : rank + 1]
    m_all = [m_mine] + [swap(m_mine, "wk", d) for d in range(1, weeks)]

    def third(*refs):
        third_kernel(cols * ni, *refs)

    state, scale_b = call(third, [(rank, rank), (1, rank)], both, got, after(gram_a, m_mine))
    inv_c, fac_b = inverse_and_unit(state, steps, raw_b, scale_b)
    scratch = [pltpu.VMEM((-(-weeks // 8) * 8, rank), jnp.float32)]
    fac_c = call(week_kernel, (1, rank), *m_all, scale_a, scale_b, inv_c, scratch=scratch)
    return (fac_a, fac_b, fac_c)


def solution(mesh):
    in_specs = (P("wk", "exp", "imp"), P("imp", None), P("wk", None))
    out_specs = (P("exp", None), P("imp", None), P("wk", None))

    return jax.shard_map(per_device, mesh=mesh, in_specs=in_specs, out_specs=out_specs, check_vma=False)
```

```python
import jax
import jax.numpy as jnp
from jax import lax
from jax.experimental import pallas as pl
from jax.experimental.pallas import tpu as pltpu
from jax.sharding import PartitionSpec as P


ridge = 0.2
eps = 1e-06
hp = lax.Precision.HIGHEST
block = 32


def dot(a, b):
    return jnp.dot(a, b, precision=hp, preferred_element_type=jnp.float32)


def spread(x, axis, i):
    return jnp.broadcast_to(x[:, i : i + 1] if axis else x[i : i + 1, :], x.shape)


def pivot_group(rows, tile, at):
    lane = lax.broadcasted_iota(jnp.int32, (8, 128), 1)
    sub = lax.broadcasted_iota(jnp.int32, (8, 128), 0)
    part = list(rows)
    own = [spread(part[tile], 1, at + q) for q in range(8)]
    raw = list(own)
    for q in range(0, 8, 2):
        c0, c1 = own[q], own[q + 1]
        a, b = spread(raw[q], 0, q), spread(raw[q + 1], 0, q)
        c, d = spread(raw[q], 0, q + 1), spread(raw[q + 1], 0, q + 1)
        inv = 1.0 / (a * d - b * c)
        t0, t1 = sub == q, sub == q + 1

        def solve(x, y, a=a, b=b, c=c, d=d, inv=inv):
            return (d * x - b * y) * inv, (a * y - c * x) * inv

        for q2 in range(q + 2, 8):
            f0, f1 = solve(spread(raw[q2], 0, q), spread(raw[q2], 0, q + 1))
            raw[q2] = (own[q2] - c0 * f0) - c1 * f1
            own[q2] = jnp.where(t0, f0, jnp.where(t1, f1, raw[q2]))
        h0, h1 = lane == at + q, lane == at + q + 1
        for t in range(len(part)):
            x, y, base = spread(part[t], 0, q), spread(part[t], 0, q + 1), part[t]
            if t == tile:
                x = jnp.where(h0, 1.0, jnp.where(h1, 0.0, x))
                y = jnp.where(h1, 1.0, jnp.where(h0, 0.0, y))
                base = jnp.where(h0 | h1, 0.0, base)
            f0, f1 = solve(x, y)
            part[t] = jnp.where(t0, f0, jnp.where(t1, f1, (base - c0 * f0) - c1 * f1))
    return part


def apply_group(target, tile, at, rows):
    lane = lax.broadcasted_iota(jnp.int32, (8, 128), 1)
    inside = (lane >= at) & (lane < at + 8)
    cols = [spread(target[tile], 1, at + q) for q in range(8)]
    out = []
    for t in range(len(target)):
        base = jnp.where(inside, 0.0, target[t]) if t == tile else target[t]
        e = [cols[q] * spread(rows[t], 0, q) for q in range(8)]
        out.append(base - (((e[0] + e[1]) + (e[2] + e[3])) + ((e[4] + e[5]) + (e[6] + e[7]))))
    return out


def apply_block(rows, width, top):
    lane = lax.broadcasted_iota(jnp.int32, rows.shape, 1)
    return jnp.where(lane < width, 0.0, rows) - dot(rows[:, :width], top)


def split(x):
    return [[x[8 * i : 8 * i + 8, 128 * t : 128 * t + 128] for t in range(x.shape[1] // 128)] for i in range(x.shape[0] // 8)]


def join(rows):
    return jnp.concatenate([jnp.concatenate(r, axis=1) for r in rows], axis=0)


def invert_square(s_ref, r_ref, t_ref):
    n, per, early = s_ref.shape[0], block // 8, 2

    def back(x):
        return pltpu.roll(x, n - block, 1)

    r_ref[...] = pltpu.roll(s_ref[block : n - block, :], block, 1)
    t_ref[...] = pltpu.roll(s_ref[n - block :, :], block, 1)

    def flush(live):
        old, top = r_ref[...], t_ref[...]
        out = lax.broadcasted_iota(jnp.int32, old.shape, 1) < jnp.where(live, block, 0)
        u = dot(jnp.where(out, old, 0.0)[:, :block], top)
        return back(jnp.where(out, 0.0, old) - u), back(top)

    def step(p, panel):
        rest, last = flush(p > 0)
        part = split(panel)
        for g in range(per):
            if g == early:
                ahead = split(apply_block(rest[:block], 8 * early, join(part[:early])))
            part[g] = pivot_group(part[g], 0, 8 * g)
            if g >= early:
                ahead = [apply_group(r, 0, 8 * g, part[g]) for r in ahead]
            for h in ([g + 1] if g + 1 < per else []) + [h for h in range(per) if h not in (g, g + 1)]:
                part[h] = apply_group(part[h], 0, 8 * g, part[g])
        r_ref[: n - 3 * block, :] = rest[block:]
        r_ref[n - 3 * block :, :] = last
        t_ref[...] = join(part)
        return back(join(ahead))

    panel = lax.fori_loop(0, n // block, step, s_ref[:block, :])
    rest, last = flush(True)
    s_ref[:block, :] = panel
    s_ref[block : n - block, :] = rest
    s_ref[n - block :, :] = last


square = [pltpu.VMEM((128, 128), jnp.float32), pltpu.VMEM((128 - 2 * block, 128), jnp.float32), pltpu.VMEM((block, 128), jnp.float32)]


def eliminate(a_ref, begin, end, *scratch):
    count = a_ref.shape[0] // 128

    def at(i):
        return pl.ds(pl.multiple_of(128 * i, 128), 128)

    def step(b, carry):
        scratch[0][...] = a_ref[at(b), at(b)]
        invert_square(*scratch)
        d = scratch[0][...]
        others = [lax.rem(b + i, count) for i in range(1, count)]
        rows = [dot(d, a_ref[at(b), at(j)]) for j in others]
        for i in others:
            left = a_ref[at(i), at(b)]
            for j, row in zip(others, rows):
                a_ref[at(i), at(j)] = a_ref[at(i), at(j)] - dot(left, row)
            a_ref[at(i), at(b)] = -dot(left, d)
        for j, row in zip(others, rows):
            a_ref[at(b), at(j)] = row
        a_ref[at(b), at(b)] = d
        return carry

    lax.fori_loop(begin, end, step, 0)


def near(x):
    return pltpu.with_memory_space_constraint(x, pltpu.VMEM)


def call(kernel, outs, *args, smem=0, scratch=()):
    specs = [pl.BlockSpec(memory_space=pltpu.SMEM)] * smem
    specs += [pl.BlockSpec(memory_space=pltpu.VMEM)] * (len(args) - smem)
    many = isinstance(outs, list)
    shapes = [pltpu.VMEM(s, jnp.float32) for s in (outs if many else [outs])]
    vmem = [pl.BlockSpec(memory_space=pltpu.VMEM)] * len(shapes)
    return pl.pallas_call(
        kernel,
        out_shape=shapes if many else shapes[0],
        in_specs=specs,
        out_specs=vmem if many else vmem[0],
        scratch_shapes=scratch,
    )(*args[:smem], *[near(a) for a in args[smem:]])


def inverse_piece(state, begin, end):
    def kernel(v_ref, o_ref, *scratch):
        o_ref[...] = v_ref[...]
        eliminate(o_ref, begin, end, *scratch)

    return call(kernel, state.shape, state, scratch=square)


def inverse_and_unit(state, begin, end, raw, scale):
    def kernel(v_ref, raw_ref, scale_ref, o_ref, unit_ref, buf, sem, *scratch):
        buf[...] = raw_ref[...] / scale_ref[...]
        copy = pltpu.make_async_copy(buf, unit_ref, sem)
        copy.start()
        o_ref[...] = v_ref[...]
        eliminate(o_ref, begin, end, *scratch)
        copy.wait()

    vmem = pl.BlockSpec(memory_space=pltpu.VMEM)
    return pl.pallas_call(
        kernel,
        out_shape=[pltpu.VMEM(state.shape, jnp.float32), jax.ShapeDtypeStruct(raw.shape, jnp.float32)],
        in_specs=[vmem] * 3,
        out_specs=[vmem, pl.BlockSpec(memory_space=pl.ANY)],
        scratch_shapes=[pltpu.VMEM(raw.shape, jnp.float32), pltpu.SemaphoreType.DMA(()), *square],
        name="inverse_unit",
    )(near(state), near(raw), near(scale))


def eye(n):
    return lax.broadcasted_iota(jnp.int32, (n, n), 0) == lax.broadcasted_iota(jnp.int32, (n, n), 1)


def outer(a, b):
    return lax.dot_general(a, b, (((0,), (0,)), ((), ())), precision=hp, preferred_element_type=jnp.float32)


def ridged(h):
    n = h.shape[0]
    on = eye(n)
    diag = jnp.where(on, h, 0.0)
    trace = jnp.sum(jnp.sum(diag, axis=0, keepdims=True), axis=1, keepdims=True)
    return h + jnp.where(on, trace * (ridge / n), 0.0)


def normalised(gram, count):
    diag = jnp.where(eye(gram.shape[0]), gram, 0.0)
    one = jnp.sqrt(jnp.sum(diag, axis=0, keepdims=True) / count + eps)
    two = jnp.sqrt(jnp.sum(diag, axis=1, keepdims=True) / count + eps)
    return one, gram * (1.0 / two) * (1.0 / one)


def after(x, *deps):
    return lax.optimization_barrier((x,) + deps)[0]


def swap(x, axis, bit):
    n = lax.axis_size(axis)
    return lax.ppermute(x, axis, [(i, i ^ bit) for i in range(n)])


def bits(axis):
    n = lax.axis_size(axis)
    return [1 << b for b in range(n.bit_length() - 1)]


def total(x, axis, some=None):
    for bit in bits(axis) if some is None else some:
        x = x + swap(x, axis, bit)
    return x


def crossed(x, axis, side, i):
    n, m = lax.axis_size(axis), lax.axis_size(side)
    one, two = bits(axis)[i], bits(axis)[-1 - i]
    pairs = [(k * m + j, (k ^ (two if j & 1 else one)) * m + j) for k in range(n) for j in range(m)]
    return lax.ppermute(x, (axis, side), pairs)


def gather_rows(x, axis):
    me = lax.axis_index(axis)
    for bit in bits(axis):
        other = swap(x, axis, bit)
        mine = (me & bit) != 0
        x = jnp.concatenate([jnp.where(mine, other, x), jnp.where(mine, x, other)], axis=0)
    return x


def open_kernel(pick_ref, f_ref, b_ref, w_ref, give_ref, row_ref, f_out_ref, b_out_ref, w_out_ref):
    f = f_ref[...]
    half = f.shape[0] // 2
    at = pl.multiple_of(pick_ref[0] * half, half)
    give_ref[:half, :] = dot(f_ref[pl.ds(at, half), :], b_ref[...] * w_ref[...])
    row = lax.dot_general(
        jnp.ones((8, f.shape[1]), jnp.float32), f, (((1,), (1,)), ((), ())), precision=hp, preferred_element_type=jnp.float32
    )[:1]
    row_ref[...] = row
    rank = give_ref.shape[1]
    give_ref[half:, :] = jnp.zeros_like(give_ref[half:, :])
    for n in range(f.shape[0] // rank):
        give_ref[half + n : half + n + 1, :] = row[:, n * rank : (n + 1) * rank]
    f_out_ref[...] = f
    b_out_ref[...] = b_ref[...]
    w_out_ref[...] = w_ref[...]


def rest_kernel(pick_ref, f_ref, b_ref, w_ref, keep_ref, small_ref, gram_ref):
    b = b_ref[...]
    half, cols = f_ref.shape[0] // 2, f_ref.shape[1]
    at = pl.multiple_of(pick_ref[0] * half, half)
    keep_ref[...] = dot(f_ref[pl.ds(at, half), :], b * w_ref[...])
    col = jnp.sum(f_ref[...], axis=0, keepdims=True)
    small_ref[...] = jnp.zeros_like(small_ref)
    small_ref[0:1, :] = dot(jnp.broadcast_to(col, (8, cols)), b)[:1]
    small_ref[1:2, :cols] = col
    small_ref[2:3, :] = jnp.broadcast_to(jnp.sum(col, axis=1, keepdims=True), (1, small_ref.shape[1]))
    gram_ref[...] = outer(b, b)


def cut_kernel(me_ref, own_ref, got_ref, row_ref, w_ref, *gives):
    half, rank = own_ref.shape
    chunk = half // len(gives)
    row = row_ref[...] + jnp.concatenate(
        [got_ref[half + n : half + n + 1, :] for n in range(row_ref.shape[1] // rank)], axis=1
    )
    for d, give in enumerate(gives):
        at = pl.multiple_of((me_ref[0] ^ d) * chunk, chunk)
        give[:chunk, :] = own_ref[pl.ds(at, chunk), :] + got_ref[pl.ds(at, chunk), :]
        give[chunk:, :] = jnp.zeros_like(give[chunk:, :])
        give[chunk : chunk + 1, :] = w_ref[...]
        for n in range(row_ref.shape[1] // rank):
            give[chunk + 1 + n : chunk + 2 + n, :] = row[:, n * rank : (n + 1) * rank]


def fold_kernel(*refs):
    *parts, heads_ref, small_ref, w_ref, give_ref, col_ref = refs
    chunk = give_ref.shape[0] - 8
    acc = parts[0][:chunk, :]
    for part in parts[1:]:
        acc = acc + part[:chunk, :]
    give_ref[:chunk, :] = acc
    grand = heads_ref[2:3, :]
    give_ref[chunk:, :] = jnp.zeros_like(give_ref[chunk:, :])
    give_ref[chunk : chunk + 1, :] = w_ref[...] * (heads_ref[0:1, :] / grand)
    cols = col_ref.shape[1]
    col_ref[...] = small_ref[1:2, :cols] / grand[:, :cols]


def first_kernel(me_ref, own_ref, other_ref, *refs):
    *parts, v_ref, gram_ref, row_ref, w_ref = refs
    rank = w_ref.shape[1]
    w_ref[...] = jnp.zeros_like(w_ref)
    row_ref[...] = jnp.zeros_like(row_ref)
    for d, part in enumerate(parts):
        chunk = part.shape[0] - 8
        at = me_ref[0] ^ d
        w_ref[pl.ds(at, 1), :] = part[chunk : chunk + 1, :]
        for n in range(row_ref.shape[1] // rank):
            row_ref[pl.ds(at, 1), n * rank : (n + 1) * rank] = part[chunk + 1 + n : chunk + 2 + n, :]
    gram = outer(w_ref[...], w_ref[...])
    gram_ref[...] = gram
    v_ref[...] = ridged((own_ref[...] + other_ref[...]) * gram)


def rows_kernel(me_ref, *refs):
    *parts, m_ref, shift_ref = refs
    shift_ref[...] = jnp.zeros_like(shift_ref)
    for d, part in enumerate(parts):
        chunk = part.shape[0] - 8
        at = me_ref[0] ^ d
        m_ref[pl.ds(pl.multiple_of(at * chunk, chunk), chunk), :] = part[:chunk, :]
        shift_ref[pl.ds(at, 1), :] = part[chunk : chunk + 1, :]


def exporter_kernel(
    me_ref, top_ref, own_ref, other_ref, row_all_ref, shift_ref, inv_ref, f_ref, col_ref, raw_ref, t_ref, m_ref, s_ref
):
    half = own_ref.shape[0]
    m_ref[pl.ds(pl.multiple_of(top_ref[0] * half, half), half), :] = own_ref[...]
    m_ref[pl.ds(pl.multiple_of((1 - top_ref[0]) * half, half), half), :] = other_ref[...]
    rank, cols = shift_ref.shape[1], f_ref.shape[1]
    s_ref[:, :rank] = shift_ref[...]
    week = lax.broadcasted_iota(jnp.int32, (s_ref.shape[0], cols), 0)
    s_ref[:, rank:] = jnp.where(week == me_ref[0], col_ref[...], 0.0)
    terms = outer(row_all_ref[...], s_ref[...])
    raw = dot(m_ref[...] - terms[:, :rank], inv_ref[...])
    raw_ref[...] = raw
    t_ref[...] = outer(f_ref[...] - terms[:, rank:], raw)


def gram_kernel(top_ref, raw_ref, g_ref):
    grams, rank = g_ref.shape
    at = pl.multiple_of(top_ref[0] * grams, grams) if grams < rank else 0
    g_ref[...] = outer(raw_ref[:, pl.ds(at, grams)], raw_ref[...])


def second_kernel(count, end, g_ref, gram_c_ref, v_ref, gram_ref, scale_ref, *scratch):
    scale, gram = normalised(g_ref[...], count)
    scale_ref[...] = scale
    gram_ref[...] = gram
    v_ref[...] = ridged(gram * gram_c_ref[...])
    eliminate(v_ref, 0, end, *scratch)


def importer_kernel(own_ref, other_ref, scale_ref, inv_ref, t_ref, raw_ref, both_ref):
    raw = dot((own_ref[...] + other_ref[...]) / scale_ref[...], inv_ref[...])
    raw_ref[...] = raw
    rank = raw.shape[1]
    both_ref[:rank, :] = outer(raw, raw)
    both_ref[rank:, :] = jnp.zeros_like(both_ref[rank:, :])
    both_ref[rank : rank + 1, :] = jnp.sum(raw * t_ref[...], axis=0, keepdims=True)


def third_kernel(count, own_ref, other_ref, gram_a_ref, v_ref, scale_ref):
    rank = own_ref.shape[1]
    scale, gram = normalised(own_ref[:rank, :] + other_ref[:rank, :], count)
    scale_ref[...] = scale
    v_ref[...] = ridged(gram * gram_a_ref[...])


def week_kernel(*refs):
    *parts, scale_a_ref, scale_b_ref, inv_ref, o_ref, s_ref = refs
    s_ref[...] = jnp.zeros_like(s_ref)
    for i, part in enumerate(parts):
        s_ref[i : i + 1, :] = part[...] / scale_a_ref[...] / scale_b_ref[...]
    raw = dot(s_ref[...], inv_ref[...])
    scale = jnp.sqrt(jnp.sum(raw * raw, axis=0, keepdims=True) / len(parts) + eps)
    o_ref[...] = raw[:1] / scale


def shares(f, b, w, top, ni):
    rows, rank = f.shape[0], w.shape[1]
    if ni == 2 and rows % rank == 0 and rows // rank <= 7:
        give, row, f, b, w = pl.pallas_call(
            open_kernel,
            out_shape=[
                pltpu.VMEM(s, jnp.float32) for s in ((rows // 2 + 8, rank), (1, rows), f.shape, b.shape, w.shape)
            ],
            in_specs=[pl.BlockSpec(memory_space=pltpu.SMEM)] + [pl.BlockSpec(memory_space=pltpu.VMEM)] * 3,
            out_specs=[pl.BlockSpec(memory_space=pltpu.VMEM)] * 5,
            name="open",
        )(1 - top, f, b, w)
        got = swap(give, "imp", 1)
        keep, small, gram = call(rest_kernel, [(rows // 2, rank), (8, rank), (rank, rank)], top, f, b, w, smem=1)
        other = swap(gram, "imp", 1)
        return f, w, keep, got, row, small, gram, other
    low = bits("imp")[:-1]
    sums = jnp.sum(f, 1)[None]
    part = jnp.concatenate([dot(f, b * w).reshape(2, rows // 2, rank), jnp.zeros((2, 8, rank))], axis=1)
    part = total(part.at[:, rows // 2 : rows // 2 + rows // rank].set(sums.reshape(-1, rank)), "imp", low)
    keep = lax.dynamic_index_in_dim(part, top[0], 0, keepdims=False)[: rows // 2]
    got = swap(lax.dynamic_index_in_dim(part, 1 - top[0], 0, keepdims=False), "imp", ni // 2)
    row = part[0, rows // 2 : rows // 2 + rows // rank].reshape(1, rows)
    col = jnp.sum(f, 0)[None]
    wide = jnp.pad(col, ((0, 0), (0, rank - col.shape[1])))
    small = jnp.concatenate([dot(col, b), wide, jnp.full((1, rank), jnp.sum(col)), jnp.zeros((5, rank))], axis=0)
    gram = total(dot(b.T, b), "imp", low)
    return f, w, keep, got, row, small, gram, swap(gram, "imp", ni // 2)


def per_device(flows, importer_factor, week_factor):
    f = flows[0]
    w = week_factor
    rank = w.shape[1]
    rows, cols = f.shape
    weeks, ni, ne = lax.axis_size("wk"), lax.axis_size("imp"), lax.axis_size("exp")
    me_k = lax.axis_index("wk").astype(jnp.int32)[None]
    top = jnp.where((lax.axis_index("imp") & (ni // 2)) != 0, 1, 0).astype(jnp.int32)[None]
    steps = rank // 128

    f, w, keep, got, row, small, gram_own, gram_other = shares(f, importer_factor, w, top, ni)
    small = small + swap(small, "exp", 1)

    chunk = keep.shape[0] // weeks
    gives = call(cut_kernel, [(chunk + 8, rank)] * weeks, me_k, keep, got, row, w, smem=1)
    got = [swap(g, "wk", d) if d else g for d, g in enumerate(gives)]
    for bit in bits("exp")[1:]:
        small = small + swap(small, "exp", bit)
    heads = total(small, "imp")
    give, col_mean = call(fold_kernel, [(chunk + 8, rank), (1, cols)], *got, heads, small, w)
    gathered = [swap(give, "wk", d) if d else give for d in range(weeks)]

    state, gram_c, row_all = call(
        first_kernel,
        [(rank, rank), (rank, rank), (-(-weeks // 8) * 8, rows)],
        me_k, after(gram_own, give), gram_other, *got,
        smem=1, scratch=[pltpu.VMEM((-(-weeks // 8) * 8, rank), jnp.float32)],
    )
    state = inverse_piece(state, 0, steps // 2)
    *gathered, state = lax.optimization_barrier((*gathered, state))
    m_rows, shifts = call(rows_kernel, [(chunk * weeks, rank), (-(-weeks // 8) * 8, rank)], me_k, *gathered, smem=1)
    m_other = swap(m_rows, "imp", ni // 2)
    inv_a = inverse_piece(state, steps // 2, steps)

    grams = rank // 2 if ni == 2 and rank % 256 == 0 else rank
    raw_a, t = call(
        exporter_kernel,
        [(rows, rank), (cols, rank)],
        me_k, top, m_rows, m_other, row_all, shifts, inv_a, f, col_mean,
        smem=2, scratch=[pltpu.VMEM((rows, rank), jnp.float32), pltpu.VMEM((-(-weeks // 8) * 8, rank + cols), jnp.float32)],
    )
    g_a = call(gram_kernel, (grams, rank), top, after(raw_a, t), smem=1)
    for i, bit in enumerate(bits("exp")):
        t_got = crossed(t, "exp", "imp", i)
        g_got = crossed(g_a, "exp", "imp", i)
        t = t + t_got
        g_a = g_a + g_got
    m_own = t * w
    m_got = swap(m_own, "wk", 1)
    g_a = gather_rows(g_a, "imp") if grams < rank else g_a

    def second(*refs):
        second_kernel(rows * ne, steps // 2, *refs)

    for bit in bits("wk")[1:]:
        m_got, g_a = lax.optimization_barrier((m_got, g_a))
        m_own = m_own + m_got
        m_got = swap(m_own, "wk", bit)
    state, gram_a, scale_a = call(
        second, [(rank, rank), (rank, rank), (1, rank)], after(g_a, m_own), gram_c, scratch=square
    )
    inv_b, fac_a = inverse_and_unit(state, steps // 2, steps, raw_a, scale_a)
    raw_b, both = call(importer_kernel, [(cols, rank), (rank + 8, rank)], m_own, m_got, scale_a, inv_b, t)
    for bit in bits("imp")[:-1]:
        both = both + swap(both, "imp", bit)
    got = swap(both, "imp", ni // 2)
    m_mine = both[rank : rank + 1] + got[rank : rank + 1]
    paired = weeks == 4 and ni == 2
    if paired:
        pairs = [(j * 4 + k, j * 4 + (k ^ (1 + j))) for k in range(4) for j in range(2)]
        near_row = lax.ppermute(m_mine, ("imp", "wk"), pairs)
        far_row = swap(m_mine, "wk", 3)
    else:
        m_all = [m_mine] + [swap(m_mine, "wk", d) for d in range(1, weeks)]

    def third(*refs):
        third_kernel(cols * ni, *refs)

    state, scale_b = call(third, [(rank, rank), (1, rank)], both, got, after(gram_a, m_mine))
    state = inverse_piece(state, 0, steps // 2)
    if paired:
        near_row, state = lax.optimization_barrier((near_row, state))
        side_row = swap(near_row, "imp", 1)
        low = lax.axis_index("imp") == 0
        m_all = [m_mine, jnp.where(low, near_row, side_row), jnp.where(low, side_row, near_row), far_row]
    inv_c, fac_b = inverse_and_unit(state, steps // 2, steps, raw_b, scale_b)
    scratch = [pltpu.VMEM((-(-weeks // 8) * 8, rank), jnp.float32)]
    fac_c = call(week_kernel, (1, rank), *m_all, scale_a, scale_b, inv_c, scratch=scratch)
    return (fac_a, fac_b, fac_c)


def solution(mesh):
    in_specs = (P("wk", "exp", "imp"), P("imp", None), P("wk", None))
    out_specs = (P("exp", None), P("imp", None), P("wk", None))

    return jax.shard_map(per_device, mesh=mesh, in_specs=in_specs, out_specs=out_specs, check_vma=False)
```

```python
import jax
import jax.numpy as jnp
from jax import lax
from jax.experimental import pallas as pl
from jax.experimental.pallas import tpu as pltpu
from jax.sharding import PartitionSpec as P


ridge = 0.2
eps = 1e-06
hp = lax.Precision.HIGHEST
block = 32


def dot(a, b):
    return jnp.dot(a, b, precision=hp, preferred_element_type=jnp.float32)


def spread(x, axis, i):
    return jnp.broadcast_to(x[:, i : i + 1] if axis else x[i : i + 1, :], x.shape)


def pivot_group(rows, tile, at):
    lane = lax.broadcasted_iota(jnp.int32, (8, 128), 1)
    sub = lax.broadcasted_iota(jnp.int32, (8, 128), 0)
    part = list(rows)
    own = [spread(part[tile], 1, at + q) for q in range(8)]
    raw = list(own)
    for q in range(0, 8, 2):
        c0, c1 = own[q], own[q + 1]
        a, b = spread(raw[q], 0, q), spread(raw[q + 1], 0, q)
        c, d = spread(raw[q], 0, q + 1), spread(raw[q + 1], 0, q + 1)
        inv = 1.0 / (a * d - b * c)
        t0, t1 = sub == q, sub == q + 1

        def solve(x, y, a=a, b=b, c=c, d=d, inv=inv):
            return (d * x - b * y) * inv, (a * y - c * x) * inv

        for q2 in range(q + 2, 8):
            f0, f1 = solve(spread(raw[q2], 0, q), spread(raw[q2], 0, q + 1))
            raw[q2] = (own[q2] - c0 * f0) - c1 * f1
            own[q2] = jnp.where(t0, f0, jnp.where(t1, f1, raw[q2]))
        h0, h1 = lane == at + q, lane == at + q + 1
        for t in range(len(part)):
            x, y, base = spread(part[t], 0, q), spread(part[t], 0, q + 1), part[t]
            if t == tile:
                x = jnp.where(h0, 1.0, jnp.where(h1, 0.0, x))
                y = jnp.where(h1, 1.0, jnp.where(h0, 0.0, y))
                base = jnp.where(h0 | h1, 0.0, base)
            f0, f1 = solve(x, y)
            part[t] = jnp.where(t0, f0, jnp.where(t1, f1, (base - c0 * f0) - c1 * f1))
    return part


def apply_group(target, tile, at, rows):
    lane = lax.broadcasted_iota(jnp.int32, (8, 128), 1)
    inside = (lane >= at) & (lane < at + 8)
    cols = [spread(target[tile], 1, at + q) for q in range(8)]
    out = []
    for t in range(len(target)):
        base = jnp.where(inside, 0.0, target[t]) if t == tile else target[t]
        e = [cols[q] * spread(rows[t], 0, q) for q in range(8)]
        out.append(base - (((e[0] + e[1]) + (e[2] + e[3])) + ((e[4] + e[5]) + (e[6] + e[7]))))
    return out


def apply_block(rows, width, top):
    lane = lax.broadcasted_iota(jnp.int32, rows.shape, 1)
    return jnp.where(lane < width, 0.0, rows) - dot(rows[:, :width], top)


def split(x):
    return [[x[8 * i : 8 * i + 8, 128 * t : 128 * t + 128] for t in range(x.shape[1] // 128)] for i in range(x.shape[0] // 8)]


def join(rows):
    return jnp.concatenate([jnp.concatenate(r, axis=1) for r in rows], axis=0)


def back(x):
    return pltpu.roll(x, x.shape[1] - block, 1)


def flush(r_ref, t_ref, live):
    old, top = r_ref[...], t_ref[...]
    out = lax.broadcasted_iota(jnp.int32, old.shape, 1) < jnp.where(live, block, 0)
    u = dot(jnp.where(out, old, 0.0)[:, :block], top)
    return back(jnp.where(out, 0.0, old) - u), back(top)


def square_steps(r_ref, t_ref, panel, begin, end):
    n, per, early = r_ref.shape[1], block // 8, 2

    def step(p, panel):
        rest, last = flush(r_ref, t_ref, p > 0)
        part = split(panel)
        for g in range(per):
            if g == early:
                ahead = split(apply_block(rest[:block], 8 * early, join(part[:early])))
            part[g] = pivot_group(part[g], 0, 8 * g)
            if g >= early:
                ahead = [apply_group(r, 0, 8 * g, part[g]) for r in ahead]
            for h in ([g + 1] if g + 1 < per else []) + [h for h in range(per) if h not in (g, g + 1)]:
                part[h] = apply_group(part[h], 0, 8 * g, part[g])
        r_ref[: n - 3 * block, :] = rest[block:]
        r_ref[n - 3 * block :, :] = last
        t_ref[...] = join(part)
        return back(join(ahead))

    return lax.fori_loop(begin, end, step, panel)


side = 128
each = side // block
held = [(side - 2 * block, side), (block, side), (block, side)]


def eliminate(a_ref, r_ref, t_ref, p_ref, begin, end):
    count = a_ref.shape[0] // side
    while begin < end:
        b, first = divmod(begin, each)
        last = min(each, first + end - begin)
        begin += last - first
        at = [slice(side * i, side * i + side) for i in range(count)]
        if first == 0:
            s = a_ref[at[b], at[b]]
            p_ref[...] = s[:block]
            r_ref[...] = pltpu.roll(s[block : side - block], block, 1)
            t_ref[...] = pltpu.roll(s[side - block :], block, 1)
        panel = square_steps(r_ref, t_ref, p_ref[...], first, last)
        p_ref[...] = panel
        if last < each:
            continue
        d = jnp.concatenate([panel, *flush(r_ref, t_ref, True)], axis=0)
        others = [i for i in range(count) if i != b]
        rows = [dot(d, a_ref[at[b], at[j]]) for j in others]
        for i in others:
            left = a_ref[at[i], at[b]]
            for j, row in zip(others, rows):
                a_ref[at[i], at[j]] = a_ref[at[i], at[j]] - dot(left, row)
            a_ref[at[i], at[b]] = -dot(left, d)
        for j, row in zip(others, rows):
            a_ref[at[b], at[j]] = row
        a_ref[at[b], at[b]] = d


def near(x):
    return pltpu.with_memory_space_constraint(x, pltpu.VMEM)


def call(kernel, outs, *args, smem=0, scratch=()):
    specs = [pl.BlockSpec(memory_space=pltpu.SMEM)] * smem
    specs += [pl.BlockSpec(memory_space=pltpu.VMEM)] * (len(args) - smem)
    many = isinstance(outs, list)
    shapes = [pltpu.VMEM(s, jnp.float32) for s in (outs if many else [outs])]
    vmem = [pl.BlockSpec(memory_space=pltpu.VMEM)] * len(shapes)
    return pl.pallas_call(
        kernel,
        out_shape=shapes if many else shapes[0],
        in_specs=specs,
        out_specs=vmem if many else vmem[0],
        scratch_shapes=scratch,
    )(*args[:smem], *[near(a) for a in args[smem:]])


def inverse_piece(state, begin, end, unit=None):
    ins, outs = len(state), 1 if end % each == 0 else 4

    def kernel(*refs):
        refs = list(refs)
        got, refs = refs[:ins], refs[ins:]
        if unit:
            (raw_ref, scale_ref), refs = refs[:2], refs[2:]
        work, refs = refs[:outs], refs[outs:]
        if unit:
            (unit_ref, buf, sem), refs = (refs[0], refs[-2], refs[-1]), refs[1:-2]
            buf[...] = raw_ref[...] / scale_ref[...]
            copy = pltpu.make_async_copy(buf, unit_ref, sem)
            copy.start()
        work = work + refs[: 4 - outs]
        for i, o in zip(got, work):
            o[...] = i[...]
        eliminate(*work, begin, end)
        if unit:
            copy.wait()

    vmem = pl.BlockSpec(memory_space=pltpu.VMEM)
    sizes = [state[0].shape] + held
    scratch = [pltpu.VMEM(x, jnp.float32) for x in sizes[outs:]]
    shapes = [pltpu.VMEM(x, jnp.float32) for x in sizes[:outs]]
    specs = [vmem] * outs
    args = list(state)
    if unit:
        args += list(unit)
        shapes.append(jax.ShapeDtypeStruct(unit[0].shape, jnp.float32))
        specs.append(pl.BlockSpec(memory_space=pl.ANY))
        scratch += [pltpu.VMEM(unit[0].shape, jnp.float32), pltpu.SemaphoreType.DMA(())]
    done = pl.pallas_call(
        kernel, out_shape=shapes, in_specs=[vmem] * len(args), out_specs=specs, scratch_shapes=scratch, name="inverse"
    )(*[near(x) for x in args])
    return (done[:outs], done[outs]) if unit else done


def eye(n):
    return lax.broadcasted_iota(jnp.int32, (n, n), 0) == lax.broadcasted_iota(jnp.int32, (n, n), 1)


def outer(a, b):
    return lax.dot_general(a, b, (((0,), (0,)), ((), ())), precision=hp, preferred_element_type=jnp.float32)


def ridged(h):
    n = h.shape[0]
    on = eye(n)
    diag = jnp.where(on, h, 0.0)
    trace = jnp.sum(jnp.sum(diag, axis=0, keepdims=True), axis=1, keepdims=True)
    return h + jnp.where(on, trace * (ridge / n), 0.0)


def normalised(gram, count):
    diag = jnp.where(eye(gram.shape[0]), gram, 0.0)
    one = jnp.sqrt(jnp.sum(diag, axis=0, keepdims=True) / count + eps)
    two = jnp.sqrt(jnp.sum(diag, axis=1, keepdims=True) / count + eps)
    return one, gram * (1.0 / two) * (1.0 / one)


def after(x, *deps):
    return lax.optimization_barrier((x,) + deps)[0]


def swap(x, axis, bit):
    n = lax.axis_size(axis)
    return lax.ppermute(x, axis, [(i, i ^ bit) for i in range(n)])


def bits(axis):
    n = lax.axis_size(axis)
    return [1 << b for b in range(n.bit_length() - 1)]


def total(x, axis, some=None):
    for bit in bits(axis) if some is None else some:
        x = x + swap(x, axis, bit)
    return x


def crossed(x, axis, side, i):
    n, m = lax.axis_size(axis), lax.axis_size(side)
    one, two = bits(axis)[i], bits(axis)[-1 - i]
    pairs = [(k * m + j, (k ^ (two if j & 1 else one)) * m + j) for k in range(n) for j in range(m)]
    return lax.ppermute(x, (axis, side), pairs)


def gather_rows(x, axis):
    me = lax.axis_index(axis)
    for bit in bits(axis):
        other = swap(x, axis, bit)
        mine = (me & bit) != 0
        x = jnp.concatenate([jnp.where(mine, other, x), jnp.where(mine, x, other)], axis=0)
    return x


def open_kernel(pick_ref, f_ref, b_ref, w_ref, give_ref, row_ref, f_out_ref, b_out_ref, w_out_ref):
    f = f_ref[...]
    half = f.shape[0] // 2
    at = pl.multiple_of(pick_ref[0] * half, half)
    give_ref[:half, :] = dot(f_ref[pl.ds(at, half), :], b_ref[...] * w_ref[...])
    row = lax.dot_general(
        jnp.ones((8, f.shape[1]), jnp.float32), f, (((1,), (1,)), ((), ())), precision=hp, preferred_element_type=jnp.float32
    )[:1]
    row_ref[...] = row
    rank = give_ref.shape[1]
    give_ref[half:, :] = jnp.zeros_like(give_ref[half:, :])
    for n in range(f.shape[0] // rank):
        give_ref[half + n : half + n + 1, :] = row[:, n * rank : (n + 1) * rank]
    f_out_ref[...] = f
    b_out_ref[...] = b_ref[...]
    w_out_ref[...] = w_ref[...]


def rest_kernel(pick_ref, f_ref, b_ref, w_ref, keep_ref, small_ref, gram_ref):
    b = b_ref[...]
    half, cols = f_ref.shape[0] // 2, f_ref.shape[1]
    at = pl.multiple_of(pick_ref[0] * half, half)
    keep_ref[...] = dot(f_ref[pl.ds(at, half), :], b * w_ref[...])
    col = jnp.sum(f_ref[...], axis=0, keepdims=True)
    small_ref[...] = jnp.zeros_like(small_ref)
    small_ref[0:1, :] = dot(jnp.broadcast_to(col, (8, cols)), b)[:1]
    small_ref[1:2, :cols] = col
    small_ref[2:3, :] = jnp.broadcast_to(jnp.sum(col, axis=1, keepdims=True), (1, small_ref.shape[1]))
    gram_ref[...] = outer(b, b)


def cut_kernel(me_ref, own_ref, got_ref, row_ref, w_ref, *gives):
    half, rank = own_ref.shape
    chunk = half // len(gives)
    row = row_ref[...] + jnp.concatenate(
        [got_ref[half + n : half + n + 1, :] for n in range(row_ref.shape[1] // rank)], axis=1
    )
    for d, give in enumerate(gives):
        at = pl.multiple_of((me_ref[0] ^ d) * chunk, chunk)
        give[:chunk, :] = own_ref[pl.ds(at, chunk), :] + got_ref[pl.ds(at, chunk), :]
        give[chunk:, :] = jnp.zeros_like(give[chunk:, :])
        give[chunk : chunk + 1, :] = w_ref[...]
        for n in range(row_ref.shape[1] // rank):
            give[chunk + 1 + n : chunk + 2 + n, :] = row[:, n * rank : (n + 1) * rank]


def fold_kernel(*refs):
    *parts, heads_ref, small_ref, w_ref, give_ref, col_ref = refs
    chunk = give_ref.shape[0] - 8
    acc = parts[0][:chunk, :]
    for part in parts[1:]:
        acc = acc + part[:chunk, :]
    give_ref[:chunk, :] = acc
    grand = heads_ref[2:3, :]
    give_ref[chunk:, :] = jnp.zeros_like(give_ref[chunk:, :])
    give_ref[chunk : chunk + 1, :] = w_ref[...] * (heads_ref[0:1, :] / grand)
    cols = col_ref.shape[1]
    col_ref[...] = small_ref[1:2, :cols] / grand[:, :cols]


def first_kernel(me_ref, own_ref, other_ref, *refs):
    *parts, v_ref, gram_ref, row_ref, w_ref = refs
    rank = w_ref.shape[1]
    w_ref[...] = jnp.zeros_like(w_ref)
    row_ref[...] = jnp.zeros_like(row_ref)
    for d, part in enumerate(parts):
        chunk = part.shape[0] - 8
        at = me_ref[0] ^ d
        w_ref[pl.ds(at, 1), :] = part[chunk : chunk + 1, :]
        for n in range(row_ref.shape[1] // rank):
            row_ref[pl.ds(at, 1), n * rank : (n + 1) * rank] = part[chunk + 1 + n : chunk + 2 + n, :]
    gram = outer(w_ref[...], w_ref[...])
    gram_ref[...] = gram
    v_ref[...] = ridged((own_ref[...] + other_ref[...]) * gram)


def rows_kernel(me_ref, *refs):
    *parts, m_ref, shift_ref = refs
    shift_ref[...] = jnp.zeros_like(shift_ref)
    for d, part in enumerate(parts):
        chunk = part.shape[0] - 8
        at = me_ref[0] ^ d
        m_ref[pl.ds(pl.multiple_of(at * chunk, chunk), chunk), :] = part[:chunk, :]
        shift_ref[pl.ds(at, 1), :] = part[chunk : chunk + 1, :]


def exporter_kernel(
    me_ref, top_ref, own_ref, other_ref, row_all_ref, shift_ref, f_ref, col_ref, m_ref, t_ref, s_ref
):
    half = own_ref.shape[0]
    m_ref[pl.ds(pl.multiple_of(top_ref[0] * half, half), half), :] = own_ref[...]
    m_ref[pl.ds(pl.multiple_of((1 - top_ref[0]) * half, half), half), :] = other_ref[...]
    rank, cols = shift_ref.shape[1], f_ref.shape[1]
    s_ref[:, :rank] = shift_ref[...]
    week = lax.broadcasted_iota(jnp.int32, (s_ref.shape[0], cols), 0)
    s_ref[:, rank:] = jnp.where(week == me_ref[0], col_ref[...], 0.0)
    terms = outer(row_all_ref[...], s_ref[...])
    m = m_ref[...] - terms[:, :rank]
    m_ref[...] = m
    t_ref[...] = outer(f_ref[...] - terms[:, rank:], m)


def raw_kernel(top_ref, m_ref, inv_ref, raw_ref, g_ref):
    raw_ref[...] = dot(m_ref[...], inv_ref[...])
    grams, rank = g_ref.shape
    at = pl.multiple_of(top_ref[0] * grams, grams) if grams < rank else 0
    g_ref[...] = outer(raw_ref[:, pl.ds(at, grams)], raw_ref[...])


def terms_kernel(own_ref, other_ref, inv_ref, w_ref, t_ref, m_ref):
    t = dot(own_ref[...] + other_ref[...], inv_ref[...])
    t_ref[...] = t
    m_ref[...] = t * w_ref[...]


def second_kernel(count, end, g_ref, gram_c_ref, v_ref, gram_ref, scale_ref, *held_refs):
    scale, gram = normalised(g_ref[...], count)
    scale_ref[...] = scale
    gram_ref[...] = gram
    v_ref[...] = ridged(gram * gram_c_ref[...])
    eliminate(v_ref, *held_refs, 0, end)


def importer_kernel(own_ref, other_ref, scale_ref, inv_ref, t_ref, raw_ref, both_ref):
    raw = dot((own_ref[...] + other_ref[...]) / scale_ref[...], inv_ref[...])
    raw_ref[...] = raw
    rank = raw.shape[1]
    both_ref[:rank, :] = outer(raw, raw)
    both_ref[rank:, :] = jnp.zeros_like(both_ref[rank:, :])
    both_ref[rank : rank + 1, :] = jnp.sum(raw * t_ref[...], axis=0, keepdims=True)


def third_kernel(count, own_ref, other_ref, gram_a_ref, v_ref, scale_ref):
    rank = own_ref.shape[1]
    scale, gram = normalised(own_ref[:rank, :] + other_ref[:rank, :], count)
    scale_ref[...] = scale
    v_ref[...] = ridged(gram * gram_a_ref[...])


def both_kernel(count, own_ref, side_ref, t_ref, t_side_ref, scale_a_ref, inv_ref, gram_a_ref, raw_ref, week_ref, v_ref, scale_ref):
    raw = dot(own_ref[...] / scale_a_ref[...], inv_ref[...])
    raw_side = dot(side_ref[...] / scale_a_ref[...], inv_ref[...])
    raw_ref[...] = raw
    week_ref[...] = jnp.sum(raw * t_ref[...], axis=0, keepdims=True) + jnp.sum(
        raw_side * t_side_ref[...], axis=0, keepdims=True
    )
    scale, gram = normalised(outer(raw, raw) + outer(raw_side, raw_side), count)
    scale_ref[...] = scale
    v_ref[...] = ridged(gram * gram_a_ref[...])


def week_kernel(*refs):
    *parts, scale_a_ref, scale_b_ref, inv_ref, o_ref, s_ref = refs
    s_ref[...] = jnp.zeros_like(s_ref)
    for i, part in enumerate(parts):
        s_ref[i : i + 1, :] = part[...] / scale_a_ref[...] / scale_b_ref[...]
    raw = dot(s_ref[...], inv_ref[...])
    scale = jnp.sqrt(jnp.sum(raw * raw, axis=0, keepdims=True) / len(parts) + eps)
    o_ref[...] = raw[:1] / scale


def shares(f, b, w, top, ni):
    rows, rank = f.shape[0], w.shape[1]
    if ni == 2 and rows % rank == 0 and rows // rank <= 7:
        give, row, f, b, w = pl.pallas_call(
            open_kernel,
            out_shape=[
                pltpu.VMEM(s, jnp.float32) for s in ((rows // 2 + 8, rank), (1, rows), f.shape, b.shape, w.shape)
            ],
            in_specs=[pl.BlockSpec(memory_space=pltpu.SMEM)] + [pl.BlockSpec(memory_space=pltpu.VMEM)] * 3,
            out_specs=[pl.BlockSpec(memory_space=pltpu.VMEM)] * 5,
            name="open",
        )(1 - top, f, b, w)
        got = swap(give, "imp", 1)
        keep, small, gram = call(rest_kernel, [(rows // 2, rank), (8, rank), (rank, rank)], top, f, b, w, smem=1)
        other = swap(gram, "imp", 1)
        return f, w, keep, got, row, small, gram, other
    low = bits("imp")[:-1]
    sums = jnp.sum(f, 1)[None]
    part = jnp.concatenate([dot(f, b * w).reshape(2, rows // 2, rank), jnp.zeros((2, 8, rank))], axis=1)
    part = total(part.at[:, rows // 2 : rows // 2 + rows // rank].set(sums.reshape(-1, rank)), "imp", low)
    keep = lax.dynamic_index_in_dim(part, top[0], 0, keepdims=False)[: rows // 2]
    got = swap(lax.dynamic_index_in_dim(part, 1 - top[0], 0, keepdims=False), "imp", ni // 2)
    row = part[0, rows // 2 : rows // 2 + rows // rank].reshape(1, rows)
    col = jnp.sum(f, 0)[None]
    wide = jnp.pad(col, ((0, 0), (0, rank - col.shape[1])))
    small = jnp.concatenate([dot(col, b), wide, jnp.full((1, rank), jnp.sum(col)), jnp.zeros((5, rank))], axis=0)
    gram = total(dot(b.T, b), "imp", low)
    return f, w, keep, got, row, small, gram, swap(gram, "imp", ni // 2)


def per_device(flows, importer_factor, week_factor):
    f = flows[0]
    w = week_factor
    rank = w.shape[1]
    rows, cols = f.shape
    weeks, ni, ne = lax.axis_size("wk"), lax.axis_size("imp"), lax.axis_size("exp")
    me_k = lax.axis_index("wk").astype(jnp.int32)[None]
    top = jnp.where((lax.axis_index("imp") & (ni // 2)) != 0, 1, 0).astype(jnp.int32)[None]
    steps = rank // block

    f, w, keep, got, row, small, gram_own, gram_other = shares(f, importer_factor, w, top, ni)
    small = small + swap(small, "exp", 1)

    chunk = keep.shape[0] // weeks
    gives = call(cut_kernel, [(chunk + 8, rank)] * weeks, me_k, keep, got, row, w, smem=1)
    got = [swap(g, "wk", d) if d else g for d, g in enumerate(gives)]
    for bit in bits("exp")[1:]:
        small = small + swap(small, "exp", bit)
    heads = total(small, "imp")
    give, col_mean = call(fold_kernel, [(chunk + 8, rank), (1, cols)], *got, heads, small, w)
    gathered = [swap(give, "wk", d) if d else give for d in range(weeks)]

    state, gram_c, row_all = call(
        first_kernel,
        [(rank, rank), (rank, rank), (-(-weeks // 8) * 8, rows)],
        me_k, after(gram_own, give), gram_other, *got,
        smem=1, scratch=[pltpu.VMEM((-(-weeks // 8) * 8, rank), jnp.float32)],
    )
    state = inverse_piece([state], 0, steps // 2)
    gathered, state = lax.optimization_barrier((gathered, state))
    m_rows, shifts = call(rows_kernel, [(chunk * weeks, rank), (-(-weeks // 8) * 8, rank)], me_k, *gathered, smem=1)
    m_other = swap(m_rows, "imp", ni // 2)
    state = inverse_piece(after(state, m_rows), steps // 2, steps * 3 // 4)
    m_other, state = lax.optimization_barrier((m_other, state))
    m_a, t = call(
        exporter_kernel,
        [(rows, rank), (cols, rank)],
        me_k, top, m_rows, m_other, row_all, shifts, f, col_mean,
        smem=2, scratch=[pltpu.VMEM((-(-weeks // 8) * 8, rank + cols), jnp.float32)],
    )
    (inv_a,) = inverse_piece(after(state, t), steps * 3 // 4, steps)
    grams = rank // 2 if ni == 2 and rank % 256 == 0 else rank
    raw_a, g_a = call(raw_kernel, [(rows, rank), (grams, rank)], top, m_a, inv_a, smem=1)

    turns = len(bits("exp"))
    for i in range(turns):
        t_got = crossed(t, "exp", "imp", i)
        if i + 1 < turns:
            t = t + t_got
    t, m_own = call(terms_kernel, [(cols, rank), (cols, rank)], t, t_got, inv_a, w)
    m_got = swap(m_own, "wk", 1)
    for i in range(turns):
        g_a = g_a + crossed(g_a, "exp", "imp", i)
    g_a = gather_rows(g_a, "imp") if grams < rank else g_a

    def second(*refs):
        second_kernel(rows * ne, steps // 2, *refs)

    for bit in bits("wk")[1:]:
        m_got, g_a = lax.optimization_barrier((m_got, g_a))
        m_own = m_own + m_got
        m_got = swap(m_own, "wk", bit)
    state, gram_a, scale_a = call(
        second,
        [(rank, rank), (rank, rank), (1, rank)],
        after(g_a, m_own), gram_c,
        scratch=[pltpu.VMEM(x, jnp.float32) for x in held],
    )
    paired = weeks == 4 and ni == 2
    if ni == 2:
        t_side = swap(t, "imp", 1)
        state, fac_a = inverse_piece([state], steps // 2, steps - 1, unit=(raw_a, scale_a))
        m_got, state = lax.optimization_barrier((m_got, state))
        m_b = m_own + m_got
        m_side = swap(m_b, "imp", 1)
        (inv_b,) = inverse_piece(after(state, m_b), steps - 1, steps)

        def both(*refs):
            both_kernel(cols * ni, *refs)

        raw_b, m_mine, state, scale_b = call(
            both,
            [(cols, rank), (1, rank), (rank, rank), (1, rank)],
            m_b, m_side, t, t_side, scale_a, inv_b, gram_a,
        )
    else:
        (inv_b,), fac_a = inverse_piece([state], steps // 2, steps, unit=(raw_a, scale_a))
        raw_b, both = call(importer_kernel, [(cols, rank), (rank + 8, rank)], m_own, m_got, scale_a, inv_b, t)
        for bit in bits("imp")[:-1]:
            both = both + swap(both, "imp", bit)
        got = swap(both, "imp", ni // 2)
        m_mine = both[rank : rank + 1] + got[rank : rank + 1]

        def third(*refs):
            third_kernel(cols * ni, *refs)

        state, scale_b = call(third, [(rank, rank), (1, rank)], both, got, gram_a)
    if paired:
        pairs = [(j * 4 + k, j * 4 + (k ^ (1 + j))) for k in range(4) for j in range(2)]
        near_row = lax.ppermute(m_mine, ("imp", "wk"), pairs)
        far_row = swap(m_mine, "wk", 3)
    else:
        m_all = [m_mine] + [swap(m_mine, "wk", d) for d in range(1, weeks)]
    state = inverse_piece([state], 0, steps // 2)
    if paired:
        near_row, state = lax.optimization_barrier((near_row, state))
        side_row = swap(near_row, "imp", 1)
        low = lax.axis_index("imp") == 0
        m_all = [m_mine, jnp.where(low, near_row, side_row), jnp.where(low, side_row, near_row), far_row]
    (inv_c,), fac_b = inverse_piece(state, steps // 2, steps, unit=(raw_b, scale_b))
    scratch = [pltpu.VMEM((-(-weeks // 8) * 8, rank), jnp.float32)]
    fac_c = call(week_kernel, (1, rank), *m_all, scale_a, scale_b, inv_c, scratch=scratch)
    return (fac_a, fac_b, fac_c)


def solution(mesh):
    in_specs = (P("wk", "exp", "imp"), P("imp", None), P("wk", None))
    out_specs = (P("exp", None), P("imp", None), P("wk", None))

    return jax.shard_map(per_device, mesh=mesh, in_specs=in_specs, out_specs=out_specs, check_vma=False)
```

```python
import jax
import jax.numpy as jnp
from jax import lax
from jax.experimental import pallas as pl
from jax.experimental.pallas import tpu as pltpu
from jax.sharding import PartitionSpec as P


ridge = 0.2
eps = 1e-06
hp = lax.Precision.HIGHEST
block = 32


def dot(a, b):
    return jnp.dot(a, b, precision=hp, preferred_element_type=jnp.float32)


def spread(x, axis, i):
    return jnp.broadcast_to(x[:, i : i + 1] if axis else x[i : i + 1, :], x.shape)


def pivot_group(rows, tile, at, own):
    lane = lax.broadcasted_iota(jnp.int32, (8, 128), 1)
    sub = lax.broadcasted_iota(jnp.int32, (8, 128), 0)
    part = list(rows)
    own, raw = list(own), list(own)
    for q in range(0, 8, 2):
        c0, c1 = own[q], own[q + 1]
        a, b = spread(raw[q], 0, q), spread(raw[q + 1], 0, q)
        c, d = spread(raw[q], 0, q + 1), spread(raw[q + 1], 0, q + 1)
        inv = 1.0 / (a * d - b * c)
        t0, t1 = sub == q, sub == q + 1

        def solve(x, y, a=a, b=b, c=c, d=d, inv=inv):
            return (d * x - b * y) * inv, (a * y - c * x) * inv

        for q2 in range(q + 2, 8):
            f0, f1 = solve(spread(raw[q2], 0, q), spread(raw[q2], 0, q + 1))
            raw[q2] = (own[q2] - c0 * f0) - c1 * f1
            own[q2] = jnp.where(t0, f0, jnp.where(t1, f1, raw[q2]))
        h0, h1 = lane == at + q, lane == at + q + 1
        for t in range(len(part)):
            x, y, base = spread(part[t], 0, q), spread(part[t], 0, q + 1), part[t]
            if t == tile:
                x = jnp.where(h0, 1.0, jnp.where(h1, 0.0, x))
                y = jnp.where(h1, 1.0, jnp.where(h0, 0.0, y))
                base = jnp.where(h0 | h1, 0.0, base)
            f0, f1 = solve(x, y)
            part[t] = jnp.where(t0, f0, jnp.where(t1, f1, (base - c0 * f0) - c1 * f1))
    return part


def apply_group(target, tile, at, rows):
    lane = lax.broadcasted_iota(jnp.int32, (8, 128), 1)
    inside = (lane >= at) & (lane < at + 8)
    cols = [spread(target[tile], 1, at + q) for q in range(8)]
    out = []
    for t in range(len(target)):
        base = jnp.where(inside, 0.0, target[t]) if t == tile else target[t]
        e = [cols[q] * spread(rows[t], 0, q) for q in range(8)]
        out.append(base - (((e[0] + e[1]) + (e[2] + e[3])) + ((e[4] + e[5]) + (e[6] + e[7]))))
    return out


def apply_block(rows, width, top):
    lane = lax.broadcasted_iota(jnp.int32, rows.shape, 1)
    return jnp.where(lane < width, 0.0, rows) - dot(rows[:, :width], top)


def split(x):
    return [[x[8 * i : 8 * i + 8, 128 * t : 128 * t + 128] for t in range(x.shape[1] // 128)] for i in range(x.shape[0] // 8)]


def join(rows):
    return jnp.concatenate([jnp.concatenate(r, axis=1) for r in rows], axis=0)


def back(x):
    return pltpu.roll(x, x.shape[1] - block, 1)


def flush(r_ref, t_ref, live):
    old, top = r_ref[...], t_ref[...]
    out = lax.broadcasted_iota(jnp.int32, old.shape, 1) < jnp.where(live, block, 0)
    u = dot(jnp.where(out, old, 0.0)[:, :block], top)
    return back(jnp.where(out, 0.0, old) - u), back(top)


def square_steps(r_ref, t_ref, panel, begin, end):
    n, per, early = r_ref.shape[1], block // 8, 2

    def columns(rows, at):
        return [spread(rows, 1, at + q) for q in range(8)]

    def step(p, carry):
        panel, *own = carry
        rest, last = flush(r_ref, t_ref, p > 0)
        part = split(panel)
        for g in range(per):
            if g == early:
                ahead = split(apply_block(rest[:block], 8 * early, join(part[:early])))
            part[g] = pivot_group(part[g], 0, 8 * g, own if g == 0 else columns(part[g][0], 8 * g))
            if g >= early:
                ahead = [apply_group(r, 0, 8 * g, part[g]) for r in ahead]
            for h in ([g + 1] if g + 1 < per else []) + [h for h in range(per) if h not in (g, g + 1)]:
                part[h] = apply_group(part[h], 0, 8 * g, part[g])
        r_ref[: n - 3 * block, :] = rest[block:]
        r_ref[n - 3 * block :, :] = last
        t_ref[...] = join(part)
        return (back(join(ahead)), *columns(ahead[0][0], block))

    return lax.fori_loop(begin, end, step, (panel, *columns(panel[:8], 0)))[0]


side = 128
each = side // block
held = [(side - 2 * block, side), (block, side), (block, side)]


def eliminate(a_ref, r_ref, t_ref, p_ref, begin, end):
    count = a_ref.shape[0] // side
    while begin < end:
        b, first = divmod(begin, each)
        last = min(each, first + end - begin)
        begin += last - first
        at = [slice(side * i, side * i + side) for i in range(count)]
        if first == 0:
            s = a_ref[at[b], at[b]]
            p_ref[...] = s[:block]
            r_ref[...] = pltpu.roll(s[block : side - block], block, 1)
            t_ref[...] = pltpu.roll(s[side - block :], block, 1)
        panel = square_steps(r_ref, t_ref, p_ref[...], first, last)
        p_ref[...] = panel
        if last < each:
            continue
        d = jnp.concatenate([panel, *flush(r_ref, t_ref, True)], axis=0)
        others = [i for i in range(count) if i != b]
        rows = [dot(d, a_ref[at[b], at[j]]) for j in others]
        for i in others:
            left = a_ref[at[i], at[b]]
            for j, row in zip(others, rows):
                a_ref[at[i], at[j]] = a_ref[at[i], at[j]] - dot(left, row)
            a_ref[at[i], at[b]] = -dot(left, d)
        for j, row in zip(others, rows):
            a_ref[at[b], at[j]] = row
        a_ref[at[b], at[b]] = d


def near(x):
    return pltpu.with_memory_space_constraint(x, pltpu.VMEM)


def call(kernel, outs, *args, smem=0, scratch=()):
    specs = [pl.BlockSpec(memory_space=pltpu.SMEM)] * smem
    specs += [pl.BlockSpec(memory_space=pltpu.VMEM)] * (len(args) - smem)
    many = isinstance(outs, list)
    shapes = [pltpu.VMEM(s, jnp.float32) for s in (outs if many else [outs])]
    vmem = [pl.BlockSpec(memory_space=pltpu.VMEM)] * len(shapes)
    return pl.pallas_call(
        kernel,
        out_shape=shapes if many else shapes[0],
        in_specs=specs,
        out_specs=vmem if many else vmem[0],
        scratch_shapes=scratch,
    )(*args[:smem], *[near(a) for a in args[smem:]])


def inverse_piece(state, begin, end, unit=None):
    ins, outs = len(state), 1 if end % each == 0 else 4

    def kernel(*refs):
        refs = list(refs)
        got, refs = refs[:ins], refs[ins:]
        if unit:
            (raw_ref, scale_ref), refs = refs[:2], refs[2:]
        work, refs = refs[:outs], refs[outs:]
        if unit:
            (unit_ref, buf, sem), refs = (refs[0], refs[-2], refs[-1]), refs[1:-2]
            buf[...] = raw_ref[...] / scale_ref[...]
            copy = pltpu.make_async_copy(buf, unit_ref, sem)
            copy.start()
        work = work + refs[: 4 - outs]
        for i, o in zip(got, work):
            o[...] = i[...]
        eliminate(*work, begin, end)
        if unit:
            copy.wait()

    vmem = pl.BlockSpec(memory_space=pltpu.VMEM)
    sizes = [state[0].shape] + held
    scratch = [pltpu.VMEM(x, jnp.float32) for x in sizes[outs:]]
    shapes = [pltpu.VMEM(x, jnp.float32) for x in sizes[:outs]]
    specs = [vmem] * outs
    args = list(state)
    if unit:
        args += list(unit)
        shapes.append(jax.ShapeDtypeStruct(unit[0].shape, jnp.float32))
        specs.append(pl.BlockSpec(memory_space=pl.ANY))
        scratch += [pltpu.VMEM(unit[0].shape, jnp.float32), pltpu.SemaphoreType.DMA(())]
    done = pl.pallas_call(
        kernel, out_shape=shapes, in_specs=[vmem] * len(args), out_specs=specs, scratch_shapes=scratch, name="inverse"
    )(*[near(x) for x in args])
    return (done[:outs], done[outs]) if unit else done


def eye(n):
    return lax.broadcasted_iota(jnp.int32, (n, n), 0) == lax.broadcasted_iota(jnp.int32, (n, n), 1)


def outer(a, b):
    return lax.dot_general(a, b, (((0,), (0,)), ((), ())), precision=hp, preferred_element_type=jnp.float32)


def ridged(h):
    n = h.shape[0]
    on = eye(n)
    diag = jnp.where(on, h, 0.0)
    trace = jnp.sum(jnp.sum(diag, axis=0, keepdims=True), axis=1, keepdims=True)
    return h + jnp.where(on, trace * (ridge / n), 0.0)


def normalised(gram, count):
    diag = jnp.where(eye(gram.shape[0]), gram, 0.0)
    one = jnp.sqrt(jnp.sum(diag, axis=0, keepdims=True) / count + eps)
    two = jnp.sqrt(jnp.sum(diag, axis=1, keepdims=True) / count + eps)
    return one, gram * (1.0 / two) * (1.0 / one)


def after(x, *deps):
    return lax.optimization_barrier((x,) + deps)[0]


def swap(x, axis, bit):
    n = lax.axis_size(axis)
    return lax.ppermute(x, axis, [(i, i ^ bit) for i in range(n)])


def bits(axis):
    n = lax.axis_size(axis)
    return [1 << b for b in range(n.bit_length() - 1)]


def total(x, axis, some=None):
    for bit in bits(axis) if some is None else some:
        x = x + swap(x, axis, bit)
    return x


def crossed(x, axis, side, i):
    n, m = lax.axis_size(axis), lax.axis_size(side)
    one, two = bits(axis)[i], bits(axis)[-1 - i]
    pairs = [(k * m + j, (k ^ (two if j & 1 else one)) * m + j) for k in range(n) for j in range(m)]
    return lax.ppermute(x, (axis, side), pairs)


def gather_rows(x, axis):
    me = lax.axis_index(axis)
    for bit in bits(axis):
        other = swap(x, axis, bit)
        mine = (me & bit) != 0
        x = jnp.concatenate([jnp.where(mine, other, x), jnp.where(mine, x, other)], axis=0)
    return x


def open_kernel(pick_ref, f_ref, b_ref, w_ref, give_ref, row_ref, f_out_ref, b_out_ref, w_out_ref):
    f = f_ref[...]
    half = f.shape[0] // 2
    at = pl.multiple_of(pick_ref[0] * half, half)
    give_ref[:half, :] = dot(f_ref[pl.ds(at, half), :], b_ref[...] * w_ref[...])
    row = lax.dot_general(
        jnp.ones((8, f.shape[1]), jnp.float32), f, (((1,), (1,)), ((), ())), precision=hp, preferred_element_type=jnp.float32
    )[:1]
    row_ref[...] = row
    rank = give_ref.shape[1]
    give_ref[half:, :] = jnp.zeros_like(give_ref[half:, :])
    for n in range(f.shape[0] // rank):
        give_ref[half + n : half + n + 1, :] = row[:, n * rank : (n + 1) * rank]
    f_out_ref[...] = f
    b_out_ref[...] = b_ref[...]
    w_out_ref[...] = w_ref[...]


def rest_kernel(pick_ref, f_ref, b_ref, w_ref, keep_ref, small_ref, gram_ref):
    b = b_ref[...]
    half, cols = f_ref.shape[0] // 2, f_ref.shape[1]
    at = pl.multiple_of(pick_ref[0] * half, half)
    keep_ref[...] = dot(f_ref[pl.ds(at, half), :], b * w_ref[...])
    col = jnp.sum(f_ref[...], axis=0, keepdims=True)
    small_ref[...] = jnp.zeros_like(small_ref)
    small_ref[0:1, :] = dot(jnp.broadcast_to(col, (8, cols)), b)[:1]
    small_ref[1:2, :cols] = col
    small_ref[2:3, :] = jnp.broadcast_to(jnp.sum(col, axis=1, keepdims=True), (1, small_ref.shape[1]))
    gram_ref[...] = outer(b, b)


def cut_kernel(me_ref, own_ref, got_ref, row_ref, w_ref, *gives):
    half, rank = own_ref.shape
    chunk = half // len(gives)
    row = row_ref[...] + jnp.concatenate(
        [got_ref[half + n : half + n + 1, :] for n in range(row_ref.shape[1] // rank)], axis=1
    )
    for d, give in enumerate(gives):
        at = pl.multiple_of((me_ref[0] ^ d) * chunk, chunk)
        give[:chunk, :] = own_ref[pl.ds(at, chunk), :] + got_ref[pl.ds(at, chunk), :]
        give[chunk:, :] = jnp.zeros_like(give[chunk:, :])
        give[chunk : chunk + 1, :] = w_ref[...]
        for n in range(row_ref.shape[1] // rank):
            give[chunk + 1 + n : chunk + 2 + n, :] = row[:, n * rank : (n + 1) * rank]


def fold_kernel(*refs):
    *parts, heads_ref, small_ref, w_ref, give_ref, col_ref = refs
    chunk = give_ref.shape[0] - 8
    acc = parts[0][:chunk, :]
    for part in parts[1:]:
        acc = acc + part[:chunk, :]
    give_ref[:chunk, :] = acc
    grand = heads_ref[2:3, :]
    give_ref[chunk:, :] = jnp.zeros_like(give_ref[chunk:, :])
    give_ref[chunk : chunk + 1, :] = w_ref[...] * (heads_ref[0:1, :] / grand)
    cols = col_ref.shape[1]
    col_ref[...] = small_ref[1:2, :cols] / grand[:, :cols]


def first_kernel(me_ref, own_ref, other_ref, *refs):
    *parts, v_ref, gram_ref, row_ref, w_ref = refs
    rank = w_ref.shape[1]
    w_ref[...] = jnp.zeros_like(w_ref)
    row_ref[...] = jnp.zeros_like(row_ref)
    for d, part in enumerate(parts):
        chunk = part.shape[0] - 8
        at = me_ref[0] ^ d
        w_ref[pl.ds(at, 1), :] = part[chunk : chunk + 1, :]
        for n in range(row_ref.shape[1] // rank):
            row_ref[pl.ds(at, 1), n * rank : (n + 1) * rank] = part[chunk + 1 + n : chunk + 2 + n, :]
    gram = outer(w_ref[...], w_ref[...])
    gram_ref[...] = gram
    v_ref[...] = ridged((own_ref[...] + other_ref[...]) * gram)


def rows_kernel(me_ref, *refs):
    *parts, m_ref, shift_ref = refs
    shift_ref[...] = jnp.zeros_like(shift_ref)
    for d, part in enumerate(parts):
        chunk = part.shape[0] - 8
        at = me_ref[0] ^ d
        m_ref[pl.ds(pl.multiple_of(at * chunk, chunk), chunk), :] = part[:chunk, :]
        shift_ref[pl.ds(at, 1), :] = part[chunk : chunk + 1, :]


def exporter_kernel(
    me_ref, top_ref, own_ref, other_ref, row_all_ref, shift_ref, f_ref, col_ref, m_ref, t_ref, s_ref
):
    half = own_ref.shape[0]
    m_ref[pl.ds(pl.multiple_of(top_ref[0] * half, half), half), :] = own_ref[...]
    m_ref[pl.ds(pl.multiple_of((1 - top_ref[0]) * half, half), half), :] = other_ref[...]
    rank, cols = shift_ref.shape[1], f_ref.shape[1]
    s_ref[:, :rank] = shift_ref[...]
    week = lax.broadcasted_iota(jnp.int32, (s_ref.shape[0], cols), 0)
    s_ref[:, rank:] = jnp.where(week == me_ref[0], col_ref[...], 0.0)
    terms = outer(row_all_ref[...], s_ref[...])
    m = m_ref[...] - terms[:, :rank]
    m_ref[...] = m
    t_ref[...] = outer(f_ref[...] - terms[:, rank:], m)


def raw_kernel(top_ref, m_ref, inv_ref, raw_ref, g_ref):
    raw_ref[...] = dot(m_ref[...], inv_ref[...])
    grams, rank = g_ref.shape
    at = pl.multiple_of(top_ref[0] * grams, grams) if grams < rank else 0
    g_ref[...] = outer(raw_ref[:, pl.ds(at, grams)], raw_ref[...])


def terms_kernel(own_ref, other_ref, inv_ref, w_ref, t_ref, m_ref):
    t = dot(own_ref[...] + other_ref[...], inv_ref[...])
    t_ref[...] = t
    m_ref[...] = t * w_ref[...]


def second_kernel(count, end, g_ref, gram_c_ref, v_ref, gram_ref, scale_ref, *held_refs):
    scale, gram = normalised(g_ref[...], count)
    scale_ref[...] = scale
    gram_ref[...] = gram
    v_ref[...] = ridged(gram * gram_c_ref[...])
    eliminate(v_ref, *held_refs, 0, end)


def importer_kernel(own_ref, other_ref, scale_ref, inv_ref, t_ref, raw_ref, both_ref):
    raw = dot((own_ref[...] + other_ref[...]) / scale_ref[...], inv_ref[...])
    raw_ref[...] = raw
    rank = raw.shape[1]
    both_ref[:rank, :] = outer(raw, raw)
    both_ref[rank:, :] = jnp.zeros_like(both_ref[rank:, :])
    both_ref[rank : rank + 1, :] = jnp.sum(raw * t_ref[...], axis=0, keepdims=True)


def third_kernel(count, own_ref, other_ref, gram_a_ref, v_ref, scale_ref):
    rank = own_ref.shape[1]
    scale, gram = normalised(own_ref[:rank, :] + other_ref[:rank, :], count)
    scale_ref[...] = scale
    v_ref[...] = ridged(gram * gram_a_ref[...])


def both_kernel(count, own_ref, side_ref, t_ref, t_side_ref, scale_a_ref, inv_ref, gram_a_ref, raw_ref, week_ref, v_ref, scale_ref):
    raw = dot(own_ref[...] / scale_a_ref[...], inv_ref[...])
    raw_side = dot(side_ref[...] / scale_a_ref[...], inv_ref[...])
    raw_ref[...] = raw
    week_ref[...] = jnp.sum(raw * t_ref[...], axis=0, keepdims=True) + jnp.sum(
        raw_side * t_side_ref[...], axis=0, keepdims=True
    )
    scale, gram = normalised(outer(raw, raw) + outer(raw_side, raw_side), count)
    scale_ref[...] = scale
    v_ref[...] = ridged(gram * gram_a_ref[...])


def week_kernel(*refs):
    *parts, scale_a_ref, scale_b_ref, inv_ref, o_ref, s_ref = refs
    s_ref[...] = jnp.zeros_like(s_ref)
    for i, part in enumerate(parts):
        s_ref[i : i + 1, :] = part[...] / scale_a_ref[...] / scale_b_ref[...]
    raw = dot(s_ref[...], inv_ref[...])
    scale = jnp.sqrt(jnp.sum(raw * raw, axis=0, keepdims=True) / len(parts) + eps)
    o_ref[...] = raw[:1] / scale


def shares(f, b, w, top, ni):
    rows, rank = f.shape[0], w.shape[1]
    if ni == 2 and rows % rank == 0 and rows // rank <= 7:
        give, row, f, b, w = pl.pallas_call(
            open_kernel,
            out_shape=[
                pltpu.VMEM(s, jnp.float32) for s in ((rows // 2 + 8, rank), (1, rows), f.shape, b.shape, w.shape)
            ],
            in_specs=[pl.BlockSpec(memory_space=pltpu.SMEM)] + [pl.BlockSpec(memory_space=pltpu.VMEM)] * 3,
            out_specs=[pl.BlockSpec(memory_space=pltpu.VMEM)] * 5,
            name="open",
        )(1 - top, f, b, w)
        got = swap(give, "imp", 1)
        keep, small, gram = call(rest_kernel, [(rows // 2, rank), (8, rank), (rank, rank)], top, f, b, w, smem=1)
        other = swap(gram, "imp", 1)
        return f, w, keep, got, row, small, gram, other
    low = bits("imp")[:-1]
    sums = jnp.sum(f, 1)[None]
    part = jnp.concatenate([dot(f, b * w).reshape(2, rows // 2, rank), jnp.zeros((2, 8, rank))], axis=1)
    part = total(part.at[:, rows // 2 : rows // 2 + rows // rank].set(sums.reshape(-1, rank)), "imp", low)
    keep = lax.dynamic_index_in_dim(part, top[0], 0, keepdims=False)[: rows // 2]
    got = swap(lax.dynamic_index_in_dim(part, 1 - top[0], 0, keepdims=False), "imp", ni // 2)
    row = part[0, rows // 2 : rows // 2 + rows // rank].reshape(1, rows)
    col = jnp.sum(f, 0)[None]
    wide = jnp.pad(col, ((0, 0), (0, rank - col.shape[1])))
    small = jnp.concatenate([dot(col, b), wide, jnp.full((1, rank), jnp.sum(col)), jnp.zeros((5, rank))], axis=0)
    gram = total(dot(b.T, b), "imp", low)
    return f, w, keep, got, row, small, gram, swap(gram, "imp", ni // 2)


def per_device(flows, importer_factor, week_factor):
    f = flows[0]
    w = week_factor
    rank = w.shape[1]
    rows, cols = f.shape
    weeks, ni, ne = lax.axis_size("wk"), lax.axis_size("imp"), lax.axis_size("exp")
    me_k = lax.axis_index("wk").astype(jnp.int32)[None]
    top = jnp.where((lax.axis_index("imp") & (ni // 2)) != 0, 1, 0).astype(jnp.int32)[None]
    steps = rank // block

    f, w, keep, got, row, small, gram_own, gram_other = shares(f, importer_factor, w, top, ni)
    small = small + swap(small, "exp", 1)

    chunk = keep.shape[0] // weeks
    gives = call(cut_kernel, [(chunk + 8, rank)] * weeks, me_k, keep, got, row, w, smem=1)
    got = [swap(g, "wk", d) if d else g for d, g in enumerate(gives)]
    for bit in bits("exp")[1:]:
        small = small + swap(small, "exp", bit)
    heads = total(small, "imp")
    give, col_mean = call(fold_kernel, [(chunk + 8, rank), (1, cols)], *got, heads, small, w)
    gathered = [swap(give, "wk", d) if d else give for d in range(weeks)]

    state, gram_c, row_all = call(
        first_kernel,
        [(rank, rank), (rank, rank), (-(-weeks // 8) * 8, rows)],
        me_k, after(gram_own, give), gram_other, *got,
        smem=1, scratch=[pltpu.VMEM((-(-weeks // 8) * 8, rank), jnp.float32)],
    )
    state = inverse_piece([state], 0, steps // 2)
    gathered, state = lax.optimization_barrier((gathered, state))
    m_rows, shifts = call(rows_kernel, [(chunk * weeks, rank), (-(-weeks // 8) * 8, rank)], me_k, *gathered, smem=1)
    m_other = swap(m_rows, "imp", ni // 2)
    state = inverse_piece(after(state, m_rows), steps // 2, steps * 3 // 4)
    m_other, state = lax.optimization_barrier((m_other, state))
    m_a, t = call(
        exporter_kernel,
        [(rows, rank), (cols, rank)],
        me_k, top, m_rows, m_other, row_all, shifts, f, col_mean,
        smem=2, scratch=[pltpu.VMEM((-(-weeks // 8) * 8, rank + cols), jnp.float32)],
    )
    (inv_a,) = inverse_piece(after(state, t), steps * 3 // 4, steps)
    grams = rank // 2 if ni == 2 and rank % 256 == 0 else rank
    raw_a, g_a = call(raw_kernel, [(rows, rank), (grams, rank)], top, m_a, inv_a, smem=1)

    turns = len(bits("exp"))
    for i in range(turns):
        t_got = crossed(t, "exp", "imp", i)
        if i + 1 < turns:
            t = t + t_got
    t, m_own = call(terms_kernel, [(cols, rank), (cols, rank)], t, t_got, inv_a, w)
    m_got = swap(m_own, "wk", 1)
    for i in range(turns):
        g_a = g_a + crossed(g_a, "exp", "imp", i)
    g_a = gather_rows(g_a, "imp") if grams < rank else g_a

    def second(*refs):
        second_kernel(rows * ne, steps // 2, *refs)

    for bit in bits("wk")[1:]:
        m_got, g_a = lax.optimization_barrier((m_got, g_a))
        m_own = m_own + m_got
        m_got = swap(m_own, "wk", bit)
    state, gram_a, scale_a = call(
        second,
        [(rank, rank), (rank, rank), (1, rank)],
        after(g_a, m_own), gram_c,
        scratch=[pltpu.VMEM(x, jnp.float32) for x in held],
    )
    paired = weeks == 4 and ni == 2
    if ni == 2:
        t_side = swap(t, "imp", 1)
        state, fac_a = inverse_piece([state], steps // 2, steps - 1, unit=(raw_a, scale_a))
        m_got, state = lax.optimization_barrier((m_got, state))
        m_b = m_own + m_got
        m_side = swap(m_b, "imp", 1)
        (inv_b,) = inverse_piece(after(state, m_b), steps - 1, steps)

        def both(*refs):
            both_kernel(cols * ni, *refs)

        raw_b, m_mine, state, scale_b = call(
            both,
            [(cols, rank), (1, rank), (rank, rank), (1, rank)],
            m_b, m_side, t, t_side, scale_a, inv_b, gram_a,
        )
    else:
        (inv_b,), fac_a = inverse_piece([state], steps // 2, steps, unit=(raw_a, scale_a))
        raw_b, both = call(importer_kernel, [(cols, rank), (rank + 8, rank)], m_own, m_got, scale_a, inv_b, t)
        for bit in bits("imp")[:-1]:
            both = both + swap(both, "imp", bit)
        got = swap(both, "imp", ni // 2)
        m_mine = both[rank : rank + 1] + got[rank : rank + 1]

        def third(*refs):
            third_kernel(cols * ni, *refs)

        state, scale_b = call(third, [(rank, rank), (1, rank)], both, got, gram_a)
    if paired:
        pairs = [(j * 4 + k, j * 4 + (k ^ (1 + j))) for k in range(4) for j in range(2)]
        far_row = swap(m_mine, "wk", 3)
        near_row = lax.ppermute(m_mine, ("imp", "wk"), pairs)
    else:
        m_all = [m_mine] + [swap(m_mine, "wk", d) for d in range(1, weeks)]
    state = inverse_piece([state], 0, steps // 2)
    if paired:
        near_row, far_row, state = lax.optimization_barrier((near_row, far_row, state))
        side_row = swap(near_row, "imp", 1)
        low = lax.axis_index("imp") == 0
        m_all = [m_mine, jnp.where(low, near_row, side_row), jnp.where(low, side_row, near_row), far_row]
    (inv_c,), fac_b = inverse_piece(state, steps // 2, steps, unit=(raw_b, scale_b))
    scratch = [pltpu.VMEM((-(-weeks // 8) * 8, rank), jnp.float32)]
    fac_c = call(week_kernel, (1, rank), *m_all, scale_a, scale_b, inv_c, scratch=scratch)
    return (fac_a, fac_b, fac_c)


def solution(mesh):
    in_specs = (P("wk", "exp", "imp"), P("imp", None), P("wk", None))
    out_specs = (P("exp", None), P("imp", None), P("wk", None))

    return jax.shard_map(per_device, mesh=mesh, in_specs=in_specs, out_specs=out_specs, check_vma=False)
```

```python
import jax
import jax.numpy as jnp
from jax import lax
from jax.experimental import pallas as pl
from jax.experimental.pallas import tpu as pltpu
from jax.sharding import PartitionSpec as P


ridge = 0.2
eps = 1e-06
hp = lax.Precision.HIGHEST
block = 32


def dot(a, b):
    return jnp.dot(a, b, precision=hp, preferred_element_type=jnp.float32)


def spread(x, axis, i):
    return jnp.broadcast_to(x[:, i : i + 1] if axis else x[i : i + 1, :], x.shape)


def pivot_group(rows, tile, at, own):
    lane = lax.broadcasted_iota(jnp.int32, (8, 128), 1)
    sub = lax.broadcasted_iota(jnp.int32, (8, 128), 0)
    part = list(rows)
    own, raw = list(own), list(own)
    for q in range(0, 8, 2):
        c0, c1 = own[q], own[q + 1]
        a, b = spread(raw[q], 0, q), spread(raw[q + 1], 0, q)
        c, d = spread(raw[q], 0, q + 1), spread(raw[q + 1], 0, q + 1)
        inv = 1.0 / (a * d - b * c)
        t0, t1 = sub == q, sub == q + 1

        def solve(x, y, a=a, b=b, c=c, d=d, inv=inv):
            return (d * x - b * y) * inv, (a * y - c * x) * inv

        for q2 in range(q + 2, 8):
            f0, f1 = solve(spread(raw[q2], 0, q), spread(raw[q2], 0, q + 1))
            raw[q2] = (own[q2] - c0 * f0) - c1 * f1
            own[q2] = jnp.where(t0, f0, jnp.where(t1, f1, raw[q2]))
        h0, h1 = lane == at + q, lane == at + q + 1
        for t in range(len(part)):
            x, y, base = spread(part[t], 0, q), spread(part[t], 0, q + 1), part[t]
            if t == tile:
                x = jnp.where(h0, 1.0, jnp.where(h1, 0.0, x))
                y = jnp.where(h1, 1.0, jnp.where(h0, 0.0, y))
                base = jnp.where(h0 | h1, 0.0, base)
            f0, f1 = solve(x, y)
            part[t] = jnp.where(t0, f0, jnp.where(t1, f1, (base - c0 * f0) - c1 * f1))
    return part


def apply_group(target, tile, at, rows):
    lane = lax.broadcasted_iota(jnp.int32, (8, 128), 1)
    inside = (lane >= at) & (lane < at + 8)
    cols = [spread(target[tile], 1, at + q) for q in range(8)]
    out = []
    for t in range(len(target)):
        base = jnp.where(inside, 0.0, target[t]) if t == tile else target[t]
        e = [cols[q] * spread(rows[t], 0, q) for q in range(8)]
        out.append(base - (((e[0] + e[1]) + (e[2] + e[3])) + ((e[4] + e[5]) + (e[6] + e[7]))))
    return out


def apply_block(rows, width, top):
    lane = lax.broadcasted_iota(jnp.int32, rows.shape, 1)
    return jnp.where(lane < width, 0.0, rows) - dot(rows[:, :width], top)


def split(x):
    return [[x[8 * i : 8 * i + 8, 128 * t : 128 * t + 128] for t in range(x.shape[1] // 128)] for i in range(x.shape[0] // 8)]


def join(rows):
    return jnp.concatenate([jnp.concatenate(r, axis=1) for r in rows], axis=0)


def back(x):
    return pltpu.roll(x, x.shape[1] - block, 1)


def flush(r_ref, t_ref, live):
    old, top = r_ref[...], t_ref[...]
    out = lax.broadcasted_iota(jnp.int32, old.shape, 1) < jnp.where(live, block, 0)
    u = dot(jnp.where(out, old, 0.0)[:, :block], top)
    return back(jnp.where(out, 0.0, old) - u), back(top)


def square_steps(r_ref, t_ref, panel, begin, end):
    n, per, early = r_ref.shape[1], block // 8, 2

    def columns(rows, at):
        return [spread(rows, 1, at + q) for q in range(8)]

    def step(p, carry):
        panel, *own = carry
        rest, last = flush(r_ref, t_ref, p > 0)
        part = split(panel)
        for g in range(per):
            if g == early:
                ahead = split(apply_block(rest[:block], 8 * early, join(part[:early])))
            part[g] = pivot_group(part[g], 0, 8 * g, own if g == 0 else columns(part[g][0], 8 * g))
            if g >= early:
                ahead = [apply_group(r, 0, 8 * g, part[g]) for r in ahead]
            for h in ([g + 1] if g + 1 < per else []) + [h for h in range(per) if h not in (g, g + 1)]:
                part[h] = apply_group(part[h], 0, 8 * g, part[g])
        r_ref[: n - 3 * block, :] = rest[block:]
        r_ref[n - 3 * block :, :] = last
        t_ref[...] = join(part)
        return (back(join(ahead)), *columns(ahead[0][0], block))

    return lax.fori_loop(begin, end, step, (panel, *columns(panel[:8], 0)))[0]


side = 128
each = side // block
held = [(side - 2 * block, side), (block, side), (block, side)]


def eliminate(a_ref, r_ref, t_ref, p_ref, begin, end):
    count = a_ref.shape[0] // side
    while begin < end:
        b, first = divmod(begin, each)
        last = min(each, first + end - begin)
        begin += last - first
        at = [slice(side * i, side * i + side) for i in range(count)]
        if first == 0:
            s = a_ref[at[b], at[b]]
            p_ref[...] = s[:block]
            r_ref[...] = pltpu.roll(s[block : side - block], block, 1)
            t_ref[...] = pltpu.roll(s[side - block :], block, 1)
        panel = square_steps(r_ref, t_ref, p_ref[...], first, last)
        p_ref[...] = panel
        if last < each:
            continue
        d = jnp.concatenate([panel, *flush(r_ref, t_ref, True)], axis=0)
        others = [i for i in range(count) if i != b]
        rows = [dot(d, a_ref[at[b], at[j]]) for j in others]
        for i in others:
            left = a_ref[at[i], at[b]]
            for j, row in zip(others, rows):
                a_ref[at[i], at[j]] = a_ref[at[i], at[j]] - dot(left, row)
            a_ref[at[i], at[b]] = -dot(left, d)
        for j, row in zip(others, rows):
            a_ref[at[b], at[j]] = row
        a_ref[at[b], at[b]] = d


def near(x):
    return pltpu.with_memory_space_constraint(x, pltpu.VMEM)


def call(kernel, outs, *args, smem=0, scratch=()):
    specs = [pl.BlockSpec(memory_space=pltpu.SMEM)] * smem
    specs += [pl.BlockSpec(memory_space=pltpu.VMEM)] * (len(args) - smem)
    many = isinstance(outs, list)
    shapes = [pltpu.VMEM(s, jnp.float32) for s in (outs if many else [outs])]
    vmem = [pl.BlockSpec(memory_space=pltpu.VMEM)] * len(shapes)
    return pl.pallas_call(
        kernel,
        out_shape=shapes if many else shapes[0],
        in_specs=specs,
        out_specs=vmem if many else vmem[0],
        scratch_shapes=scratch,
    )(*args[:smem], *[near(a) for a in args[smem:]])


def inverse_piece(state, begin, end, unit=None):
    ins, outs = len(state), 1 if end % each == 0 else 4

    def kernel(*refs):
        refs = list(refs)
        got, refs = refs[:ins], refs[ins:]
        if unit:
            (raw_ref, scale_ref), refs = refs[:2], refs[2:]
        work, refs = refs[:outs], refs[outs:]
        if unit:
            (unit_ref, buf, sem), refs = (refs[0], refs[-2], refs[-1]), refs[1:-2]
            buf[...] = raw_ref[...] / scale_ref[...]
            copy = pltpu.make_async_copy(buf, unit_ref, sem)
            copy.start()
        work = work + refs[: 4 - outs]
        for i, o in zip(got, work):
            o[...] = i[...]
        eliminate(*work, begin, end)
        if unit:
            copy.wait()

    vmem = pl.BlockSpec(memory_space=pltpu.VMEM)
    sizes = [state[0].shape] + held
    scratch = [pltpu.VMEM(x, jnp.float32) for x in sizes[outs:]]
    shapes = [pltpu.VMEM(x, jnp.float32) for x in sizes[:outs]]
    specs = [vmem] * outs
    args = list(state)
    if unit:
        args += list(unit)
        shapes.append(jax.ShapeDtypeStruct(unit[0].shape, jnp.float32))
        specs.append(pl.BlockSpec(memory_space=pl.ANY))
        scratch += [pltpu.VMEM(unit[0].shape, jnp.float32), pltpu.SemaphoreType.DMA(())]
    done = pl.pallas_call(
        kernel, out_shape=shapes, in_specs=[vmem] * len(args), out_specs=specs, scratch_shapes=scratch, name="inverse"
    )(*[near(x) for x in args])
    return (done[:outs], done[outs]) if unit else done


def eye(n):
    return lax.broadcasted_iota(jnp.int32, (n, n), 0) == lax.broadcasted_iota(jnp.int32, (n, n), 1)


def outer(a, b):
    return lax.dot_general(a, b, (((0,), (0,)), ((), ())), precision=hp, preferred_element_type=jnp.float32)


def ridged(h):
    n = h.shape[0]
    on = eye(n)
    diag = jnp.where(on, h, 0.0)
    trace = jnp.sum(jnp.sum(diag, axis=0, keepdims=True), axis=1, keepdims=True)
    return h + jnp.where(on, trace * (ridge / n), 0.0)


def normalised(gram, count):
    diag = jnp.where(eye(gram.shape[0]), gram, 0.0)
    one = jnp.sqrt(jnp.sum(diag, axis=0, keepdims=True) / count + eps)
    two = jnp.sqrt(jnp.sum(diag, axis=1, keepdims=True) / count + eps)
    return one, gram * (1.0 / two) * (1.0 / one)


def after(x, *deps):
    return lax.optimization_barrier((x,) + deps)[0]


def swap(x, axis, bit):
    n = lax.axis_size(axis)
    return lax.ppermute(x, axis, [(i, i ^ bit) for i in range(n)])


def bits(axis):
    n = lax.axis_size(axis)
    return [1 << b for b in range(n.bit_length() - 1)]


def total(x, axis, some=None):
    for bit in bits(axis) if some is None else some:
        x = x + swap(x, axis, bit)
    return x


def crossed(x, axis, side, i):
    n, m = lax.axis_size(axis), lax.axis_size(side)
    one, two = bits(axis)[i], bits(axis)[-1 - i]
    pairs = [(k * m + j, (k ^ (two if j & 1 else one)) * m + j) for k in range(n) for j in range(m)]
    return lax.ppermute(x, (axis, side), pairs)


def gather_rows(x, axis):
    me = lax.axis_index(axis)
    for bit in bits(axis):
        other = swap(x, axis, bit)
        mine = (me & bit) != 0
        x = jnp.concatenate([jnp.where(mine, other, x), jnp.where(mine, x, other)], axis=0)
    return x


def core_rows(f_ref, core, week):
    half = f_ref.shape[0] // 2
    chunk = half // 4
    at = [(0, week ^ (1 + core)), (1, week ^ (1 + core)), (core, week ^ 3), (core, week)]
    return jnp.concatenate(
        [f_ref[pl.ds(pl.multiple_of(h * half + q * chunk, chunk), chunk), :] for h, q in at], axis=0
    )


def open_kernel(core_ref, week_ref, f_ref, b_ref, w_ref, give_ref, row_ref, f_out_ref, b_out_ref, w_out_ref):
    f = f_ref[...]
    half = f.shape[0] // 2
    give_ref[:half, :] = dot(core_rows(f_ref, 1 - core_ref[0], week_ref[0]), b_ref[...] * w_ref[...])
    row = lax.dot_general(
        jnp.ones((8, f.shape[1]), jnp.float32), f, (((1,), (1,)), ((), ())), precision=hp, preferred_element_type=jnp.float32
    )[:1]
    row_ref[...] = row
    rank = give_ref.shape[1]
    give_ref[half:, :] = jnp.zeros_like(give_ref[half:, :])
    for n in range(f.shape[0] // rank):
        give_ref[half + n : half + n + 1, :] = row[:, n * rank : (n + 1) * rank]
    f_out_ref[...] = f
    b_out_ref[...] = b_ref[...]
    w_out_ref[...] = w_ref[...]


def rest_kernel(core_ref, week_ref, f_ref, b_ref, w_ref, keep_ref, small_ref, gram_ref):
    b = b_ref[...]
    cols = f_ref.shape[1]
    keep_ref[...] = dot(core_rows(f_ref, core_ref[0], week_ref[0]), b * w_ref[...])
    col = jnp.sum(f_ref[...], axis=0, keepdims=True)
    small_ref[...] = jnp.zeros_like(small_ref)
    small_ref[0:1, :] = dot(jnp.broadcast_to(col, (8, cols)), b)[:1]
    small_ref[1:2, :cols] = col
    small_ref[2:3, :] = jnp.broadcast_to(jnp.sum(col, axis=1, keepdims=True), (1, small_ref.shape[1]))
    gram_ref[...] = outer(b, b)


def cut_kernel(me_ref, own_ref, got_ref, row_ref, w_ref, *gives):
    half, rank = own_ref.shape
    chunk = half // len(gives)
    row = row_ref[...] + jnp.concatenate(
        [got_ref[half + n : half + n + 1, :] for n in range(row_ref.shape[1] // rank)], axis=1
    )
    for d, give in enumerate(gives):
        at = pl.multiple_of((me_ref[0] ^ d) * chunk, chunk)
        give[:chunk, :] = own_ref[pl.ds(at, chunk), :] + got_ref[pl.ds(at, chunk), :]
        give[chunk:, :] = jnp.zeros_like(give[chunk:, :])
        give[chunk : chunk + 1, :] = w_ref[...]
        for n in range(row_ref.shape[1] // rank):
            give[chunk + 1 + n : chunk + 2 + n, :] = row[:, n * rank : (n + 1) * rank]


def cut_pair_kernel(own_ref, got_ref, row_ref, w_ref, near_ref, far_ref, mine_ref):
    half, rank = own_ref.shape
    chunk = half // 4
    row = row_ref[...] + jnp.concatenate(
        [got_ref[half + n : half + n + 1, :] for n in range(row_ref.shape[1] // rank)], axis=1
    )
    x = own_ref[...] + got_ref[:half, :]
    for out, part in ((near_ref, x[: 2 * chunk]), (far_ref, x[2 * chunk : 3 * chunk]), (mine_ref, x[3 * chunk :])):
        m = part.shape[0]
        out[:m, :] = part
        out[m:, :] = jnp.zeros_like(out[m:, :])
        out[m : m + 1, :] = w_ref[...]
        for n in range(row_ref.shape[1] // rank):
            out[m + 1 + n : m + 2 + n, :] = row[:, n * rank : (n + 1) * rank]


def mix_kernel(near_ref, far_ref, mine_ref, out_ref):
    chunk = mine_ref.shape[0] - 8
    out_ref[: 2 * chunk, :] = near_ref[: 2 * chunk, :]
    out_ref[2 * chunk : 3 * chunk, :] = far_ref[:chunk, :] + mine_ref[:chunk, :]
    out_ref[3 * chunk :, :] = near_ref[2 * chunk :, :]


def fold_pair_kernel(core_ref, mix_ref, side_ref, heads_ref, small_ref, w_ref, pair_ref, own_ref, col_ref):
    chunk = own_ref.shape[0] - 8
    core = core_ref[0]
    for h in range(2):
        own = mix_ref[2 * chunk : 3 * chunk, :]
        other = side_ref[2 * chunk : 3 * chunk, :]
        at = slice(h * chunk, (h + 1) * chunk)
        pair_ref[at, :] = (mix_ref[at, :] + side_ref[at, :]) + jnp.where(core == h, own, other)
    own_ref[:chunk, :] = pair_ref[pl.ds(pl.multiple_of(core * chunk, chunk), chunk), :]
    grand = heads_ref[2:3, :]
    for out in (pair_ref, own_ref):
        m = out.shape[0] - 8
        out[m:, :] = jnp.zeros_like(out[m:, :])
        out[m : m + 1, :] = w_ref[...] * (heads_ref[0:1, :] / grand)
    cols = col_ref.shape[1]
    col_ref[...] = small_ref[1:2, :cols] / grand[:, :cols]


def week_at(week, core, d):
    if core is None:
        return week ^ d
    return week ^ (0, 1 + core, 2 - core, 3)[d]


def rows_pair_kernel(core_ref, week_ref, pair_ref, near_ref, side_ref, far_ref, far_side_ref, m_ref, shift_ref):
    chunk, half = far_ref.shape[0] - 8, m_ref.shape[0] // 2
    shift_ref[...] = jnp.zeros_like(shift_ref)
    for d, part in enumerate((pair_ref, near_ref, side_ref, far_ref)):
        m = part.shape[0] - 8
        shift_ref[pl.ds(week_at(week_ref[0], core_ref[0], d), 1), :] = part[m : m + 1, :]
    for h in range(2):
        for d, part in enumerate((pair_ref, near_ref, side_ref)):
            at = pl.multiple_of(h * half + week_at(week_ref[0], core_ref[0], d) * chunk, chunk)
            m_ref[pl.ds(at, chunk), :] = part[h * chunk : (h + 1) * chunk, :]
        at = pl.multiple_of(h * half + week_at(week_ref[0], core_ref[0], 3) * chunk, chunk)
        m_ref[pl.ds(at, chunk), :] = jnp.where(core_ref[0] == h, far_ref[:chunk, :], far_side_ref[:chunk, :])


def fold_kernel(*refs):
    *parts, heads_ref, small_ref, w_ref, give_ref, col_ref = refs
    chunk = give_ref.shape[0] - 8
    acc = parts[0][:chunk, :]
    for part in parts[1:]:
        acc = acc + part[:chunk, :]
    give_ref[:chunk, :] = acc
    grand = heads_ref[2:3, :]
    give_ref[chunk:, :] = jnp.zeros_like(give_ref[chunk:, :])
    give_ref[chunk : chunk + 1, :] = w_ref[...] * (heads_ref[0:1, :] / grand)
    cols = col_ref.shape[1]
    col_ref[...] = small_ref[1:2, :cols] / grand[:, :cols]


def first_kernel(paired, core_ref, week_ref, own_ref, other_ref, *refs):
    *parts, v_ref, gram_ref, row_ref, w_ref = refs
    rank = w_ref.shape[1]
    w_ref[...] = jnp.zeros_like(w_ref)
    row_ref[...] = jnp.zeros_like(row_ref)
    for d, part in enumerate(parts):
        chunk = part.shape[0] - 8
        at = week_at(week_ref[0], core_ref[0] if paired else None, d)
        w_ref[pl.ds(at, 1), :] = part[chunk : chunk + 1, :]
        for n in range(row_ref.shape[1] // rank):
            row_ref[pl.ds(at, 1), n * rank : (n + 1) * rank] = part[chunk + 1 + n : chunk + 2 + n, :]
    gram = outer(w_ref[...], w_ref[...])
    gram_ref[...] = gram
    v_ref[...] = ridged((own_ref[...] + other_ref[...]) * gram)


def rows_kernel(me_ref, *refs):
    *parts, m_ref, shift_ref = refs
    shift_ref[...] = jnp.zeros_like(shift_ref)
    for d, part in enumerate(parts):
        chunk = part.shape[0] - 8
        at = me_ref[0] ^ d
        m_ref[pl.ds(pl.multiple_of(at * chunk, chunk), chunk), :] = part[:chunk, :]
        shift_ref[pl.ds(at, 1), :] = part[chunk : chunk + 1, :]


def exporter_kernel(
    me_ref, sum_ref, row_all_ref, shift_ref, f_ref, col_ref, m_ref, t_ref, s_ref
):
    rank, cols = shift_ref.shape[1], f_ref.shape[1]
    s_ref[:, :rank] = shift_ref[...]
    week = lax.broadcasted_iota(jnp.int32, (s_ref.shape[0], cols), 0)
    s_ref[:, rank:] = jnp.where(week == me_ref[0], col_ref[...], 0.0)
    terms = outer(row_all_ref[...], s_ref[...])
    m = sum_ref[...] - terms[:, :rank]
    m_ref[...] = m
    t_ref[...] = outer(f_ref[...] - terms[:, rank:], m)


def raw_kernel(top_ref, m_ref, inv_ref, raw_ref, g_ref):
    raw_ref[...] = dot(m_ref[...], inv_ref[...])
    grams, rank = g_ref.shape
    at = pl.multiple_of(top_ref[0] * grams, grams) if grams < rank else 0
    g_ref[...] = outer(raw_ref[:, pl.ds(at, grams)], raw_ref[...])


def terms_kernel(own_ref, other_ref, inv_ref, w_ref, t_ref, m_ref):
    t = dot(own_ref[...] + other_ref[...], inv_ref[...])
    t_ref[...] = t
    m_ref[...] = t * w_ref[...]


def second_kernel(count, end, g_ref, gram_c_ref, v_ref, gram_ref, scale_ref, *held_refs):
    scale, gram = normalised(g_ref[...], count)
    scale_ref[...] = scale
    gram_ref[...] = gram
    v_ref[...] = ridged(gram * gram_c_ref[...])
    eliminate(v_ref, *held_refs, 0, end)


def importer_kernel(own_ref, other_ref, scale_ref, inv_ref, t_ref, raw_ref, both_ref):
    raw = dot((own_ref[...] + other_ref[...]) / scale_ref[...], inv_ref[...])
    raw_ref[...] = raw
    rank = raw.shape[1]
    both_ref[:rank, :] = outer(raw, raw)
    both_ref[rank:, :] = jnp.zeros_like(both_ref[rank:, :])
    both_ref[rank : rank + 1, :] = jnp.sum(raw * t_ref[...], axis=0, keepdims=True)


def third_kernel(count, own_ref, other_ref, gram_a_ref, v_ref, scale_ref):
    rank = own_ref.shape[1]
    scale, gram = normalised(own_ref[:rank, :] + other_ref[:rank, :], count)
    scale_ref[...] = scale
    v_ref[...] = ridged(gram * gram_a_ref[...])


def both_kernel(count, own_ref, side_ref, t_ref, t_side_ref, scale_a_ref, inv_ref, gram_a_ref, raw_ref, week_ref, v_ref, scale_ref):
    raw = dot(own_ref[...] / scale_a_ref[...], inv_ref[...])
    raw_side = dot(side_ref[...] / scale_a_ref[...], inv_ref[...])
    raw_ref[...] = raw
    week_ref[...] = jnp.sum(raw * t_ref[...], axis=0, keepdims=True) + jnp.sum(
        raw_side * t_side_ref[...], axis=0, keepdims=True
    )
    scale, gram = normalised(outer(raw, raw) + outer(raw_side, raw_side), count)
    scale_ref[...] = scale
    v_ref[...] = ridged(gram * gram_a_ref[...])


def week_kernel(*refs):
    *parts, scale_a_ref, scale_b_ref, inv_ref, o_ref, s_ref = refs
    s_ref[...] = jnp.zeros_like(s_ref)
    for i, part in enumerate(parts):
        s_ref[i : i + 1, :] = part[...] / scale_a_ref[...] / scale_b_ref[...]
    raw = dot(s_ref[...], inv_ref[...])
    scale = jnp.sqrt(jnp.sum(raw * raw, axis=0, keepdims=True) / len(parts) + eps)
    o_ref[...] = raw[:1] / scale


def shares_pair(f, b, w, core, week):
    rows, rank = f.shape[0], w.shape[1]
    give, row, f, b, w = pl.pallas_call(
        open_kernel,
        out_shape=[
            pltpu.VMEM(s, jnp.float32) for s in ((rows // 2 + 8, rank), (1, rows), f.shape, b.shape, w.shape)
        ],
        in_specs=[pl.BlockSpec(memory_space=pltpu.SMEM)] * 2 + [pl.BlockSpec(memory_space=pltpu.VMEM)] * 3,
        out_specs=[pl.BlockSpec(memory_space=pltpu.VMEM)] * 5,
        name="open",
    )(core, week, f, b, w)
    got = swap(give, "imp", 1)
    keep, small, gram = call(rest_kernel, [(rows // 2, rank), (8, rank), (rank, rank)], core, week, f, b, w, smem=2)
    other = swap(gram, "imp", 1)
    return f, w, keep, got, row, small, gram, other


def shares(f, b, w, top, ni):
    rows, rank = f.shape[0], w.shape[1]
    low = bits("imp")[:-1]
    sums = jnp.sum(f, 1)[None]
    part = jnp.concatenate([dot(f, b * w).reshape(2, rows // 2, rank), jnp.zeros((2, 8, rank))], axis=1)
    part = total(part.at[:, rows // 2 : rows // 2 + rows // rank].set(sums.reshape(-1, rank)), "imp", low)
    keep = lax.dynamic_index_in_dim(part, top[0], 0, keepdims=False)[: rows // 2]
    got = swap(lax.dynamic_index_in_dim(part, 1 - top[0], 0, keepdims=False), "imp", ni // 2)
    row = part[0, rows // 2 : rows // 2 + rows // rank].reshape(1, rows)
    col = jnp.sum(f, 0)[None]
    wide = jnp.pad(col, ((0, 0), (0, rank - col.shape[1])))
    small = jnp.concatenate([dot(col, b), wide, jnp.full((1, rank), jnp.sum(col)), jnp.zeros((5, rank))], axis=0)
    gram = total(dot(b.T, b), "imp", low)
    return f, w, keep, got, row, small, gram, swap(gram, "imp", ni // 2)


def per_device(flows, importer_factor, week_factor):
    f = flows[0]
    w = week_factor
    rank = w.shape[1]
    rows, cols = f.shape
    weeks, ni, ne = lax.axis_size("wk"), lax.axis_size("imp"), lax.axis_size("exp")
    me_k = lax.axis_index("wk").astype(jnp.int32)[None]
    top = jnp.where((lax.axis_index("imp") & (ni // 2)) != 0, 1, 0).astype(jnp.int32)[None]
    steps = rank // block

    chunk = rows // 2 // weeks
    paired = ni == 2 and weeks == 4 and rows % rank == 0 and rows // rank <= 7 and chunk % 8 == 0
    tall = -(-weeks // 8) * 8
    if paired:
        f, w, keep, got, row, small, gram_own, gram_other = shares_pair(f, importer_factor, w, top, me_k)
    else:
        f, w, keep, got, row, small, gram_own, gram_other = shares(f, importer_factor, w, top, ni)
    small = small + swap(small, "exp", 1)

    def near_weeks(x):
        pairs = [(j * 4 + k, j * 4 + (k ^ (1 + j))) for k in range(4) for j in range(2)]
        return lax.ppermute(x, ("imp", "wk"), pairs)

    if paired:
        give_near, give_far, mine = call(
            cut_pair_kernel, [(2 * chunk + 8, rank), (chunk + 8, rank), (chunk + 8, rank)], keep, got, row, w
        )
        got_far = swap(give_far, "wk", 3)
        got_near = near_weeks(give_near)
    else:
        gives = call(cut_kernel, [(chunk + 8, rank)] * weeks, me_k, keep, got, row, w, smem=1)
        got = [swap(g, "wk", d) if d else g for d, g in enumerate(gives)]
    for bit in bits("exp")[1:]:
        small = small + swap(small, "exp", bit)
    heads = total(small, "imp")
    if paired:
        got_near, got_far, heads = lax.optimization_barrier((got_near, got_far, heads))
        mix = call(mix_kernel, (3 * chunk + 8, rank), got_near, got_far, mine)
        side_mix = swap(mix, "imp", 1)
        got = [mine, mix, side_mix, got_far]
        pair, give, col_mean = call(
            fold_pair_kernel,
            [(2 * chunk + 8, rank), (chunk + 8, rank), (1, cols)],
            top, mix, side_mix, heads, small, w,
            smem=1,
        )
        far = swap(give, "wk", 3)
        near_rows = near_weeks(pair)
        gathered = [near_rows, far]
    else:
        give, col_mean = call(fold_kernel, [(chunk + 8, rank), (1, cols)], *got, heads, small, w)
        gathered = [swap(give, "wk", d) if d else give for d in range(weeks)]

    def first(*refs):
        first_kernel(paired, *refs)

    state, gram_c, row_all = call(
        first,
        [(rank, rank), (rank, rank), (tall, rows)],
        top, me_k, after(gram_own, give), gram_other, *got,
        smem=2, scratch=[pltpu.VMEM((tall, rank), jnp.float32)],
    )
    state = inverse_piece([state], 0, steps // 2)
    if paired:
        cut = steps
        state = inverse_piece(state, steps // 2, steps * 7 // 8)
        near_rows, far, state = lax.optimization_barrier((*gathered, state))
        near_side, far_side = swap(near_rows, "imp", 1), swap(far, "imp", 1)
        state = inverse_piece(after(state, near_rows), steps * 7 // 8, steps)
        near_side, far_side, state = lax.optimization_barrier((near_side, far_side, state))
        m_rows, shifts = call(
            rows_pair_kernel, [(rows, rank), (tall, rank)],
            top, me_k, pair, near_rows, near_side, far, far_side,
            smem=2,
        )
    else:
        cut = steps * 3 // 4
        gathered, state = lax.optimization_barrier((gathered, state))
        m_rows, shifts = call(rows_kernel, [(chunk * weeks, rank), (tall, rank)], me_k, *gathered, smem=1)
        m_other = swap(m_rows, "imp", ni // 2)
        state = inverse_piece(after(state, m_rows), steps // 2, cut)
        m_other, state = lax.optimization_barrier((m_other, state))
        upper = top[0] != 0
        m_rows = jnp.concatenate([jnp.where(upper, m_other, m_rows), jnp.where(upper, m_rows, m_other)], axis=0)
    m_a, t = call(
        exporter_kernel,
        [(rows, rank), (cols, rank)],
        me_k, m_rows, row_all, shifts, f, col_mean,
        smem=1, scratch=[pltpu.VMEM((tall, rank + cols), jnp.float32)],
    )
    (inv_a,) = inverse_piece(after(state, t), cut, steps) if cut < steps else state
    grams = rank // 2 if ni == 2 and rank % 256 == 0 else rank
    raw_a, g_a = call(raw_kernel, [(rows, rank), (grams, rank)], top, m_a, inv_a, smem=1)

    turns = len(bits("exp"))
    for i in range(turns):
        t_got = crossed(t, "exp", "imp", i)
        if i + 1 < turns:
            t = t + t_got
    t, m_own = call(terms_kernel, [(cols, rank), (cols, rank)], t, t_got, inv_a, w)
    m_got = swap(m_own, "wk", 1)
    for i in range(turns):
        g_a = g_a + crossed(g_a, "exp", "imp", i)
    g_a = gather_rows(g_a, "imp") if grams < rank else g_a

    def second(*refs):
        second_kernel(rows * ne, 1, *refs)

    v, gram_a, scale_a, *state = call(second, [(rank, rank), (rank, rank), (1, rank)] + held, after(g_a, m_own), gram_c)
    for bit in bits("wk")[1:]:
        m_got, v = lax.optimization_barrier((m_got, v))
        m_own = m_own + m_got
        m_got = swap(m_own, "wk", bit)
    state = [after(v, m_own), *state]
    if ni == 2:
        t_side = swap(t, "imp", 1)
        state, fac_a = inverse_piece(state, 1, steps - 1, unit=(raw_a, scale_a))
        m_got, *state = lax.optimization_barrier((m_got, *state))
        m_b = m_own + m_got
        m_side = swap(m_b, "imp", 1)
        (inv_b,) = inverse_piece([after(state[0], m_b), *state[1:]], steps - 1, steps)

        def both(*refs):
            both_kernel(cols * ni, *refs)

        raw_b, m_mine, state, scale_b = call(
            both,
            [(cols, rank), (1, rank), (rank, rank), (1, rank)],
            m_b, m_side, t, t_side, scale_a, inv_b, gram_a,
        )
    else:
        (inv_b,), fac_a = inverse_piece(state, 1, steps, unit=(raw_a, scale_a))
        raw_b, both = call(importer_kernel, [(cols, rank), (rank + 8, rank)], m_own, m_got, scale_a, inv_b, t)
        for bit in bits("imp")[:-1]:
            both = both + swap(both, "imp", bit)
        got = swap(both, "imp", ni // 2)
        m_mine = both[rank : rank + 1] + got[rank : rank + 1]

        def third(*refs):
            third_kernel(cols * ni, *refs)

        state, scale_b = call(third, [(rank, rank), (1, rank)], both, got, gram_a)
    if paired:
        far_row = swap(m_mine, "wk", 3)
        near_row = near_weeks(m_mine)
    else:
        m_all = [m_mine] + [swap(m_mine, "wk", d) for d in range(1, weeks)]
    state = inverse_piece([state], 0, steps // 2)
    if paired:
        near_row, far_row, state = lax.optimization_barrier((near_row, far_row, state))
        side_row = swap(near_row, "imp", 1)
        low = lax.axis_index("imp") == 0
        m_all = [m_mine, jnp.where(low, near_row, side_row), jnp.where(low, side_row, near_row), far_row]
    (inv_c,), fac_b = inverse_piece(state, steps // 2, steps, unit=(raw_b, scale_b))
    scratch = [pltpu.VMEM((-(-weeks // 8) * 8, rank), jnp.float32)]
    fac_c = call(week_kernel, (1, rank), *m_all, scale_a, scale_b, inv_c, scratch=scratch)
    return (fac_a, fac_b, fac_c)


def solution(mesh):
    in_specs = (P("wk", "exp", "imp"), P("imp", None), P("wk", None))
    out_specs = (P("exp", None), P("imp", None), P("wk", None))

    return jax.shard_map(per_device, mesh=mesh, in_specs=in_specs, out_specs=out_specs, check_vma=False)
```

```python
import jax
import jax.numpy as jnp
from jax import lax
from jax.experimental import pallas as pl
from jax.experimental.pallas import tpu as pltpu
from jax.sharding import PartitionSpec as P


ridge = 0.2
eps = 1e-06
hp = lax.Precision.HIGHEST
block = 32


def dot(a, b):
    return jnp.dot(a, b, precision=hp, preferred_element_type=jnp.float32)


def spread(x, axis, i):
    return jnp.broadcast_to(x[:, i : i + 1] if axis else x[i : i + 1, :], x.shape)


def pivot_group(rows, tile, at, own):
    lane = lax.broadcasted_iota(jnp.int32, (8, 128), 1)
    sub = lax.broadcasted_iota(jnp.int32, (8, 128), 0)
    part = list(rows)
    own, raw = list(own), list(own)
    for q in range(0, 8, 2):
        c0, c1 = own[q], own[q + 1]
        a, b = spread(raw[q], 0, q), spread(raw[q + 1], 0, q)
        c, d = spread(raw[q], 0, q + 1), spread(raw[q + 1], 0, q + 1)
        inv = 1.0 / (a * d - b * c)
        t0, t1 = sub == q, sub == q + 1

        def solve(x, y, a=a, b=b, c=c, d=d, inv=inv):
            return (d * x - b * y) * inv, (a * y - c * x) * inv

        for q2 in range(q + 2, 8):
            f0, f1 = solve(spread(raw[q2], 0, q), spread(raw[q2], 0, q + 1))
            raw[q2] = (own[q2] - c0 * f0) - c1 * f1
            own[q2] = jnp.where(t0, f0, jnp.where(t1, f1, raw[q2]))
        h0, h1 = lane == at + q, lane == at + q + 1
        for t in range(len(part)):
            x, y, base = spread(part[t], 0, q), spread(part[t], 0, q + 1), part[t]
            if t == tile:
                x = jnp.where(h0, 1.0, jnp.where(h1, 0.0, x))
                y = jnp.where(h1, 1.0, jnp.where(h0, 0.0, y))
                base = jnp.where(h0 | h1, 0.0, base)
            f0, f1 = solve(x, y)
            part[t] = jnp.where(t0, f0, jnp.where(t1, f1, (base - c0 * f0) - c1 * f1))
    return part


def apply_group(target, tile, at, rows):
    lane = lax.broadcasted_iota(jnp.int32, (8, 128), 1)
    inside = (lane >= at) & (lane < at + 8)
    cols = [spread(target[tile], 1, at + q) for q in range(8)]
    out = []
    for t in range(len(target)):
        base = jnp.where(inside, 0.0, target[t]) if t == tile else target[t]
        e = [cols[q] * spread(rows[t], 0, q) for q in range(8)]
        out.append(base - (((e[0] + e[1]) + (e[2] + e[3])) + ((e[4] + e[5]) + (e[6] + e[7]))))
    return out


def apply_block(rows, width, top):
    lane = lax.broadcasted_iota(jnp.int32, rows.shape, 1)
    return jnp.where(lane < width, 0.0, rows) - dot(rows[:, :width], top)


def split(x):
    return [[x[8 * i : 8 * i + 8, 128 * t : 128 * t + 128] for t in range(x.shape[1] // 128)] for i in range(x.shape[0] // 8)]


def join(rows):
    return jnp.concatenate([jnp.concatenate(r, axis=1) for r in rows], axis=0)


def back(x):
    return pltpu.roll(x, x.shape[1] - block, 1)


def flush(r_ref, t_ref, live):
    old, top = r_ref[...], t_ref[...]
    out = lax.broadcasted_iota(jnp.int32, old.shape, 1) < jnp.where(live, block, 0)
    u = dot(jnp.where(out, old, 0.0)[:, :block], top)
    return back(jnp.where(out, 0.0, old) - u), back(top)


def square_steps(r_ref, t_ref, panel, begin, end):
    n, per, early = r_ref.shape[1], block // 8, 2

    def columns(rows, at):
        return [spread(rows, 1, at + q) for q in range(8)]

    def step(p, carry):
        panel, *own = carry
        rest, last = flush(r_ref, t_ref, p > 0)
        part = split(panel)
        for g in range(per):
            if g == early:
                ahead = split(apply_block(rest[:block], 8 * early, join(part[:early])))
            part[g] = pivot_group(part[g], 0, 8 * g, own if g == 0 else columns(part[g][0], 8 * g))
            if g >= early:
                ahead = [apply_group(r, 0, 8 * g, part[g]) for r in ahead]
            for h in ([g + 1] if g + 1 < per else []) + [h for h in range(per) if h not in (g, g + 1)]:
                part[h] = apply_group(part[h], 0, 8 * g, part[g])
        r_ref[: n - 3 * block, :] = rest[block:]
        r_ref[n - 3 * block :, :] = last
        t_ref[...] = join(part)
        return (back(join(ahead)), *columns(ahead[0][0], block))

    twice = 2 if (end - begin) % 2 == 0 else 1
    return lax.fori_loop(begin, end, step, (panel, *columns(panel[:8], 0)), unroll=twice)[0]


side = 128
each = side // block
held = [(side - 2 * block, side), (block, side), (block, side)]


def eliminate(a_ref, r_ref, t_ref, p_ref, begin, end):
    count = a_ref.shape[0] // side
    while begin < end:
        b, first = divmod(begin, each)
        last = min(each, first + end - begin)
        begin += last - first
        at = [slice(side * i, side * i + side) for i in range(count)]
        if first == 0:
            s = a_ref[at[b], at[b]]
            p_ref[...] = s[:block]
            r_ref[...] = pltpu.roll(s[block : side - block], block, 1)
            t_ref[...] = pltpu.roll(s[side - block :], block, 1)
        panel = square_steps(r_ref, t_ref, p_ref[...], first, last)
        p_ref[...] = panel
        if last < each:
            continue
        d = jnp.concatenate([panel, *flush(r_ref, t_ref, True)], axis=0)
        others = [i for i in range(count) if i != b]
        rows = [dot(d, a_ref[at[b], at[j]]) for j in others]
        for i in others:
            left = a_ref[at[i], at[b]]
            for j, row in zip(others, rows):
                a_ref[at[i], at[j]] = a_ref[at[i], at[j]] - dot(left, row)
            a_ref[at[i], at[b]] = -dot(left, d)
        for j, row in zip(others, rows):
            a_ref[at[b], at[j]] = row
        a_ref[at[b], at[b]] = d


def near(x):
    return pltpu.with_memory_space_constraint(x, pltpu.VMEM)


def call(kernel, outs, *args, smem=0, scratch=()):
    specs = [pl.BlockSpec(memory_space=pltpu.SMEM)] * smem
    specs += [pl.BlockSpec(memory_space=pltpu.VMEM)] * (len(args) - smem)
    many = isinstance(outs, list)
    shapes = [pltpu.VMEM(s, jnp.float32) for s in (outs if many else [outs])]
    vmem = [pl.BlockSpec(memory_space=pltpu.VMEM)] * len(shapes)
    return pl.pallas_call(
        kernel,
        out_shape=shapes if many else shapes[0],
        in_specs=specs,
        out_specs=vmem if many else vmem[0],
        scratch_shapes=scratch,
    )(*args[:smem], *[near(a) for a in args[smem:]])


def inverse_piece(state, begin, end, unit=None):
    ins, outs = len(state), 1 if end % each == 0 else 4

    def kernel(*refs):
        refs = list(refs)
        got, refs = refs[:ins], refs[ins:]
        if unit:
            (raw_ref, scale_ref), refs = refs[:2], refs[2:]
        work, refs = refs[:outs], refs[outs:]
        if unit:
            (unit_ref, buf, sem), refs = (refs[0], refs[-2], refs[-1]), refs[1:-2]
            buf[...] = raw_ref[...] / scale_ref[...]
            copy = pltpu.make_async_copy(buf, unit_ref, sem)
            copy.start()
        work = work + refs[: 4 - outs]
        for i, o in zip(got, work):
            o[...] = i[...]
        eliminate(*work, begin, end)
        if unit:
            copy.wait()

    vmem = pl.BlockSpec(memory_space=pltpu.VMEM)
    sizes = [state[0].shape] + held
    scratch = [pltpu.VMEM(x, jnp.float32) for x in sizes[outs:]]
    shapes = [pltpu.VMEM(x, jnp.float32) for x in sizes[:outs]]
    specs = [vmem] * outs
    args = list(state)
    if unit:
        args += list(unit)
        shapes.append(jax.ShapeDtypeStruct(unit[0].shape, jnp.float32))
        specs.append(pl.BlockSpec(memory_space=pl.ANY))
        scratch += [pltpu.VMEM(unit[0].shape, jnp.float32), pltpu.SemaphoreType.DMA(())]
    done = pl.pallas_call(
        kernel, out_shape=shapes, in_specs=[vmem] * len(args), out_specs=specs, scratch_shapes=scratch, name="inverse"
    )(*[near(x) for x in args])
    return (done[:outs], done[outs]) if unit else done


def eye(n):
    return lax.broadcasted_iota(jnp.int32, (n, n), 0) == lax.broadcasted_iota(jnp.int32, (n, n), 1)


def outer(a, b):
    return lax.dot_general(a, b, (((0,), (0,)), ((), ())), precision=hp, preferred_element_type=jnp.float32)


def ridged(h):
    n = h.shape[0]
    on = eye(n)
    diag = jnp.where(on, h, 0.0)
    trace = jnp.sum(jnp.sum(diag, axis=0, keepdims=True), axis=1, keepdims=True)
    unit = 1.0 / (trace / n)
    return h * unit + jnp.where(on, ridge, 0.0), unit


def normalised(gram, count):
    diag = jnp.where(eye(gram.shape[0]), gram, 0.0)
    one = jnp.sqrt(jnp.sum(diag, axis=0, keepdims=True) / count + eps)
    two = jnp.sqrt(jnp.sum(diag, axis=1, keepdims=True) / count + eps)
    return one, gram * (1.0 / two) * (1.0 / one)


def after(x, *deps):
    return lax.optimization_barrier((x,) + deps)[0]


def swap(x, axis, bit):
    n = lax.axis_size(axis)
    return lax.ppermute(x, axis, [(i, i ^ bit) for i in range(n)])


def bits(axis):
    n = lax.axis_size(axis)
    return [1 << b for b in range(n.bit_length() - 1)]


def total(x, axis, some=None):
    for bit in bits(axis) if some is None else some:
        x = x + swap(x, axis, bit)
    return x


def crossed(x, axis, side, i):
    n, m = lax.axis_size(axis), lax.axis_size(side)
    one, two = bits(axis)[i], bits(axis)[-1 - i]
    pairs = [(k * m + j, (k ^ (two if j & 1 else one)) * m + j) for k in range(n) for j in range(m)]
    return lax.ppermute(x, (axis, side), pairs)


def gather_rows(x, axis):
    me = lax.axis_index(axis)
    for bit in bits(axis):
        other = swap(x, axis, bit)
        mine = (me & bit) != 0
        x = jnp.concatenate([jnp.where(mine, other, x), jnp.where(mine, x, other)], axis=0)
    return x


def core_rows(f_ref, core, week):
    half = f_ref.shape[0] // 2
    chunk = half // 4
    at = [(0, week ^ (1 + core)), (1, week ^ (1 + core)), (core, week ^ 3), (core, week)]
    return jnp.concatenate(
        [f_ref[pl.ds(pl.multiple_of(h * half + q * chunk, chunk), chunk), :] for h, q in at], axis=0
    )


def open_kernel(core_ref, week_ref, f_ref, b_ref, w_ref, give_ref, row_ref, f_out_ref, b_out_ref, w_out_ref):
    f = f_ref[...]
    half = f.shape[0] // 2
    give_ref[:half, :] = dot(core_rows(f_ref, 1 - core_ref[0], week_ref[0]), b_ref[...] * w_ref[...])
    row = lax.dot_general(
        jnp.ones((8, f.shape[1]), jnp.float32), f, (((1,), (1,)), ((), ())), precision=hp, preferred_element_type=jnp.float32
    )[:1]
    row_ref[...] = row
    rank = give_ref.shape[1]
    give_ref[half:, :] = jnp.zeros_like(give_ref[half:, :])
    for n in range(f.shape[0] // rank):
        give_ref[half + n : half + n + 1, :] = row[:, n * rank : (n + 1) * rank]
    f_out_ref[...] = f
    b_out_ref[...] = b_ref[...]
    w_out_ref[...] = w_ref[...]


def rest_kernel(core_ref, week_ref, f_ref, b_ref, w_ref, keep_ref, small_ref, gram_ref):
    b = b_ref[...]
    cols = f_ref.shape[1]
    keep_ref[...] = dot(core_rows(f_ref, core_ref[0], week_ref[0]), b * w_ref[...])
    col = jnp.sum(f_ref[...], axis=0, keepdims=True)
    small_ref[...] = jnp.zeros_like(small_ref)
    small_ref[0:1, :] = dot(jnp.broadcast_to(col, (8, cols)), b)[:1]
    small_ref[1:2, :cols] = col
    small_ref[2:3, :] = jnp.broadcast_to(jnp.sum(col, axis=1, keepdims=True), (1, small_ref.shape[1]))
    gram_ref[...] = outer(b, b)


def cut_kernel(me_ref, own_ref, got_ref, row_ref, w_ref, *gives):
    half, rank = own_ref.shape
    chunk = half // len(gives)
    row = row_ref[...] + jnp.concatenate(
        [got_ref[half + n : half + n + 1, :] for n in range(row_ref.shape[1] // rank)], axis=1
    )
    for d, give in enumerate(gives):
        at = pl.multiple_of((me_ref[0] ^ d) * chunk, chunk)
        give[:chunk, :] = own_ref[pl.ds(at, chunk), :] + got_ref[pl.ds(at, chunk), :]
        give[chunk:, :] = jnp.zeros_like(give[chunk:, :])
        give[chunk : chunk + 1, :] = w_ref[...]
        for n in range(row_ref.shape[1] // rank):
            give[chunk + 1 + n : chunk + 2 + n, :] = row[:, n * rank : (n + 1) * rank]


def cut_pair_kernel(own_ref, got_ref, row_ref, w_ref, near_ref, far_ref, mine_ref):
    half, rank = own_ref.shape
    chunk = half // 4
    row = row_ref[...] + jnp.concatenate(
        [got_ref[half + n : half + n + 1, :] for n in range(row_ref.shape[1] // rank)], axis=1
    )
    x = own_ref[...] + got_ref[:half, :]
    for out, part in ((near_ref, x[: 2 * chunk]), (far_ref, x[2 * chunk : 3 * chunk]), (mine_ref, x[3 * chunk :])):
        m = part.shape[0]
        out[:m, :] = part
        out[m:, :] = jnp.zeros_like(out[m:, :])
        out[m : m + 1, :] = w_ref[...]
        for n in range(row_ref.shape[1] // rank):
            out[m + 1 + n : m + 2 + n, :] = row[:, n * rank : (n + 1) * rank]


def mix_kernel(near_ref, far_ref, mine_ref, out_ref):
    chunk = mine_ref.shape[0] - 8
    out_ref[: 2 * chunk, :] = near_ref[: 2 * chunk, :]
    out_ref[2 * chunk : 3 * chunk, :] = far_ref[:chunk, :] + mine_ref[:chunk, :]
    out_ref[3 * chunk :, :] = near_ref[2 * chunk :, :]


def fold_pair_kernel(core_ref, mix_ref, side_ref, heads_ref, small_ref, w_ref, pair_ref, own_ref, col_ref):
    chunk = own_ref.shape[0] - 8
    core = core_ref[0]
    for h in range(2):
        own = mix_ref[2 * chunk : 3 * chunk, :]
        other = side_ref[2 * chunk : 3 * chunk, :]
        at = slice(h * chunk, (h + 1) * chunk)
        pair_ref[at, :] = (mix_ref[at, :] + side_ref[at, :]) + jnp.where(core == h, own, other)
    own_ref[:chunk, :] = pair_ref[pl.ds(pl.multiple_of(core * chunk, chunk), chunk), :]
    grand = heads_ref[2:3, :]
    for out in (pair_ref, own_ref):
        m = out.shape[0] - 8
        out[m:, :] = jnp.zeros_like(out[m:, :])
        out[m : m + 1, :] = w_ref[...] * (heads_ref[0:1, :] / grand)
    cols = col_ref.shape[1]
    col_ref[...] = small_ref[1:2, :cols] / grand[:, :cols]


def week_at(week, core, d):
    if core is None:
        return week ^ d
    return week ^ (0, 1 + core, 2 - core, 3)[d]


def rows_pair_kernel(core_ref, week_ref, pair_ref, near_ref, side_ref, far_ref, far_side_ref, m_ref, shift_ref):
    chunk, half = far_ref.shape[0] - 8, m_ref.shape[0] // 2
    shift_ref[...] = jnp.zeros_like(shift_ref)
    for d, part in enumerate((pair_ref, near_ref, side_ref, far_ref)):
        m = part.shape[0] - 8
        shift_ref[pl.ds(week_at(week_ref[0], core_ref[0], d), 1), :] = part[m : m + 1, :]
    for h in range(2):
        for d, part in enumerate((pair_ref, near_ref, side_ref)):
            at = pl.multiple_of(h * half + week_at(week_ref[0], core_ref[0], d) * chunk, chunk)
            m_ref[pl.ds(at, chunk), :] = part[h * chunk : (h + 1) * chunk, :]
        at = pl.multiple_of(h * half + week_at(week_ref[0], core_ref[0], 3) * chunk, chunk)
        m_ref[pl.ds(at, chunk), :] = jnp.where(core_ref[0] == h, far_ref[:chunk, :], far_side_ref[:chunk, :])


def fold_kernel(*refs):
    *parts, heads_ref, small_ref, w_ref, give_ref, col_ref = refs
    chunk = give_ref.shape[0] - 8
    acc = parts[0][:chunk, :]
    for part in parts[1:]:
        acc = acc + part[:chunk, :]
    give_ref[:chunk, :] = acc
    grand = heads_ref[2:3, :]
    give_ref[chunk:, :] = jnp.zeros_like(give_ref[chunk:, :])
    give_ref[chunk : chunk + 1, :] = w_ref[...] * (heads_ref[0:1, :] / grand)
    cols = col_ref.shape[1]
    col_ref[...] = small_ref[1:2, :cols] / grand[:, :cols]


def first_kernel(paired, core_ref, week_ref, own_ref, other_ref, *refs):
    *parts, v_ref, gram_ref, row_ref, unit_ref, w_ref = refs
    rank = w_ref.shape[1]
    w_ref[...] = jnp.zeros_like(w_ref)
    row_ref[...] = jnp.zeros_like(row_ref)
    for d, part in enumerate(parts):
        chunk = part.shape[0] - 8
        at = week_at(week_ref[0], core_ref[0] if paired else None, d)
        w_ref[pl.ds(at, 1), :] = part[chunk : chunk + 1, :]
        for n in range(row_ref.shape[1] // rank):
            row_ref[pl.ds(at, 1), n * rank : (n + 1) * rank] = part[chunk + 1 + n : chunk + 2 + n, :]
    gram = outer(w_ref[...], w_ref[...])
    gram_ref[...] = gram
    v_ref[...], unit = ridged((own_ref[...] + other_ref[...]) * gram)
    unit_ref[...] = jnp.broadcast_to(unit, unit_ref.shape)


def rows_kernel(me_ref, *refs):
    *parts, m_ref, shift_ref = refs
    shift_ref[...] = jnp.zeros_like(shift_ref)
    for d, part in enumerate(parts):
        chunk = part.shape[0] - 8
        at = me_ref[0] ^ d
        m_ref[pl.ds(pl.multiple_of(at * chunk, chunk), chunk), :] = part[:chunk, :]
        shift_ref[pl.ds(at, 1), :] = part[chunk : chunk + 1, :]


def exporter_kernel(
    me_ref, sum_ref, row_all_ref, shift_ref, f_ref, col_ref, m_ref, t_ref, s_ref
):
    rank, cols = shift_ref.shape[1], f_ref.shape[1]
    s_ref[:, :rank] = shift_ref[...]
    week = lax.broadcasted_iota(jnp.int32, (s_ref.shape[0], cols), 0)
    s_ref[:, rank:] = jnp.where(week == me_ref[0], col_ref[...], 0.0)
    terms = outer(row_all_ref[...], s_ref[...])
    m = sum_ref[...] - terms[:, :rank]
    m_ref[...] = m
    t_ref[...] = outer(f_ref[...] - terms[:, rank:], m)


def raw_kernel(top_ref, m_ref, inv_ref, unit_ref, raw_ref, g_ref):
    raw_ref[...] = dot(m_ref[...], inv_ref[...]) * unit_ref[...]
    grams, rank = g_ref.shape
    at = pl.multiple_of(top_ref[0] * grams, grams) if grams < rank else 0
    g_ref[...] = outer(raw_ref[:, pl.ds(at, grams)], raw_ref[...])


def terms_kernel(own_ref, other_ref, inv_ref, unit_ref, w_ref, t_ref, m_ref):
    t = dot(own_ref[...] + other_ref[...], inv_ref[...]) * unit_ref[...]
    t_ref[...] = t
    m_ref[...] = t * w_ref[...]


def second_kernel(count, end, g_ref, gram_c_ref, v_ref, gram_ref, scale_ref, unit_ref, *held_refs):
    scale, gram = normalised(g_ref[...], count)
    scale_ref[...] = scale
    gram_ref[...] = gram
    v_ref[...], unit = ridged(gram * gram_c_ref[...])
    unit_ref[...] = jnp.broadcast_to(unit, unit_ref.shape)
    eliminate(v_ref, *held_refs, 0, end)


def importer_kernel(own_ref, other_ref, scale_ref, inv_ref, unit_ref, t_ref, raw_ref, both_ref):
    raw = dot((own_ref[...] + other_ref[...]) / scale_ref[...], inv_ref[...]) * unit_ref[...]
    raw_ref[...] = raw
    rank = raw.shape[1]
    both_ref[:rank, :] = outer(raw, raw)
    both_ref[rank:, :] = jnp.zeros_like(both_ref[rank:, :])
    both_ref[rank : rank + 1, :] = jnp.sum(raw * t_ref[...], axis=0, keepdims=True)


def third_kernel(count, own_ref, other_ref, gram_a_ref, v_ref, scale_ref, unit_ref):
    rank = own_ref.shape[1]
    scale, gram = normalised(own_ref[:rank, :] + other_ref[:rank, :], count)
    scale_ref[...] = scale
    v_ref[...], unit = ridged(gram * gram_a_ref[...])
    unit_ref[...] = jnp.broadcast_to(unit, unit_ref.shape)


def both_kernel(count, *refs):
    own_ref, side_ref, t_ref, t_side_ref, scale_a_ref, inv_ref, unit_b_ref, gram_a_ref, *outs = refs
    raw_ref, week_ref, v_ref, scale_ref, unit_ref = outs
    raw = dot(own_ref[...] / scale_a_ref[...], inv_ref[...]) * unit_b_ref[...]
    raw_side = dot(side_ref[...] / scale_a_ref[...], inv_ref[...]) * unit_b_ref[...]
    raw_ref[...] = raw
    week_ref[...] = jnp.sum(raw * t_ref[...], axis=0, keepdims=True) + jnp.sum(
        raw_side * t_side_ref[...], axis=0, keepdims=True
    )
    scale, gram = normalised(outer(raw, raw) + outer(raw_side, raw_side), count)
    scale_ref[...] = scale
    v_ref[...], unit = ridged(gram * gram_a_ref[...])
    unit_ref[...] = jnp.broadcast_to(unit, unit_ref.shape)


def week_kernel(*refs):
    *parts, scale_a_ref, scale_b_ref, inv_ref, unit_ref, o_ref, s_ref = refs
    s_ref[...] = jnp.zeros_like(s_ref)
    for i, part in enumerate(parts):
        s_ref[i : i + 1, :] = part[...] / scale_a_ref[...] / scale_b_ref[...]
    raw = dot(s_ref[...], inv_ref[...]) * unit_ref[...]
    scale = jnp.sqrt(jnp.sum(raw * raw, axis=0, keepdims=True) / len(parts) + eps)
    o_ref[...] = raw[:1] / scale


def shares_pair(f, b, w, core, week):
    rows, rank = f.shape[0], w.shape[1]
    give, row, f, b, w = pl.pallas_call(
        open_kernel,
        out_shape=[
            pltpu.VMEM(s, jnp.float32) for s in ((rows // 2 + 8, rank), (1, rows), f.shape, b.shape, w.shape)
        ],
        in_specs=[pl.BlockSpec(memory_space=pltpu.SMEM)] * 2 + [pl.BlockSpec(memory_space=pltpu.VMEM)] * 3,
        out_specs=[pl.BlockSpec(memory_space=pltpu.VMEM)] * 5,
        name="open",
    )(core, week, f, b, w)
    got = swap(give, "imp", 1)
    keep, small, gram = call(rest_kernel, [(rows // 2, rank), (8, rank), (rank, rank)], core, week, f, b, w, smem=2)
    other = swap(gram, "imp", 1)
    return f, w, keep, got, row, small, gram, other


def shares(f, b, w, top, ni):
    rows, rank = f.shape[0], w.shape[1]
    low = bits("imp")[:-1]
    sums = jnp.sum(f, 1)[None]
    part = jnp.concatenate([dot(f, b * w).reshape(2, rows // 2, rank), jnp.zeros((2, 8, rank))], axis=1)
    part = total(part.at[:, rows // 2 : rows // 2 + rows // rank].set(sums.reshape(-1, rank)), "imp", low)
    keep = lax.dynamic_index_in_dim(part, top[0], 0, keepdims=False)[: rows // 2]
    got = swap(lax.dynamic_index_in_dim(part, 1 - top[0], 0, keepdims=False), "imp", ni // 2)
    row = part[0, rows // 2 : rows // 2 + rows // rank].reshape(1, rows)
    col = jnp.sum(f, 0)[None]
    wide = jnp.pad(col, ((0, 0), (0, rank - col.shape[1])))
    small = jnp.concatenate([dot(col, b), wide, jnp.full((1, rank), jnp.sum(col)), jnp.zeros((5, rank))], axis=0)
    gram = total(dot(b.T, b), "imp", low)
    return f, w, keep, got, row, small, gram, swap(gram, "imp", ni // 2)


def per_device(flows, importer_factor, week_factor):
    f = flows[0]
    w = week_factor
    rank = w.shape[1]
    rows, cols = f.shape
    weeks, ni, ne = lax.axis_size("wk"), lax.axis_size("imp"), lax.axis_size("exp")
    me_k = lax.axis_index("wk").astype(jnp.int32)[None]
    top = jnp.where((lax.axis_index("imp") & (ni // 2)) != 0, 1, 0).astype(jnp.int32)[None]
    steps = rank // block

    chunk = rows // 2 // weeks
    paired = ni == 2 and weeks == 4 and rows % rank == 0 and rows // rank <= 7 and chunk % 8 == 0
    tall = -(-weeks // 8) * 8
    if paired:
        f, w, keep, got, row, small, gram_own, gram_other = shares_pair(f, importer_factor, w, top, me_k)
    else:
        f, w, keep, got, row, small, gram_own, gram_other = shares(f, importer_factor, w, top, ni)
    small = small + swap(small, "exp", 1)

    def near_weeks(x):
        pairs = [(j * 4 + k, j * 4 + (k ^ (1 + j))) for k in range(4) for j in range(2)]
        return lax.ppermute(x, ("imp", "wk"), pairs)

    if paired:
        give_near, give_far, mine = call(
            cut_pair_kernel, [(2 * chunk + 8, rank), (chunk + 8, rank), (chunk + 8, rank)], keep, got, row, w
        )
        got_far = swap(give_far, "wk", 3)
        got_near = near_weeks(give_near)
    else:
        gives = call(cut_kernel, [(chunk + 8, rank)] * weeks, me_k, keep, got, row, w, smem=1)
        got = [swap(g, "wk", d) if d else g for d, g in enumerate(gives)]
    for bit in bits("exp")[1:]:
        small = small + swap(small, "exp", bit)
    heads = total(small, "imp")
    if paired:
        got_near, got_far, heads = lax.optimization_barrier((got_near, got_far, heads))
        mix = call(mix_kernel, (3 * chunk + 8, rank), got_near, got_far, mine)
        side_mix = swap(mix, "imp", 1)
        got = [mine, mix, side_mix, got_far]
        pair, give, col_mean = call(
            fold_pair_kernel,
            [(2 * chunk + 8, rank), (chunk + 8, rank), (1, cols)],
            top, mix, side_mix, heads, small, w,
            smem=1,
        )
        far = swap(give, "wk", 3)
        near_rows = near_weeks(pair)
        gathered = [near_rows, far]
    else:
        give, col_mean = call(fold_kernel, [(chunk + 8, rank), (1, cols)], *got, heads, small, w)
        gathered = [swap(give, "wk", d) if d else give for d in range(weeks)]

    def first(*refs):
        first_kernel(paired, *refs)

    state, gram_c, row_all, unit_a = call(
        first,
        [(rank, rank), (rank, rank), (tall, rows), (1, rank)],
        top, me_k, after(gram_own, give), gram_other, *got,
        smem=2, scratch=[pltpu.VMEM((tall, rank), jnp.float32)],
    )
    state = inverse_piece([state], 0, steps // 2)
    if paired:
        cut = steps
        state = inverse_piece(state, steps // 2, steps * 7 // 8)
        near_rows, far, state = lax.optimization_barrier((*gathered, state))
        near_side, far_side = swap(near_rows, "imp", 1), swap(far, "imp", 1)
        state = inverse_piece(after(state, near_rows), steps * 7 // 8, steps)
        near_side, far_side, state = lax.optimization_barrier((near_side, far_side, state))
        m_rows, shifts = call(
            rows_pair_kernel, [(rows, rank), (tall, rank)],
            top, me_k, pair, near_rows, near_side, far, far_side,
            smem=2,
        )
    else:
        cut = steps * 3 // 4
        gathered, state = lax.optimization_barrier((gathered, state))
        m_rows, shifts = call(rows_kernel, [(chunk * weeks, rank), (tall, rank)], me_k, *gathered, smem=1)
        m_other = swap(m_rows, "imp", ni // 2)
        state = inverse_piece(after(state, m_rows), steps // 2, cut)
        m_other, state = lax.optimization_barrier((m_other, state))
        upper = top[0] != 0
        m_rows = jnp.concatenate([jnp.where(upper, m_other, m_rows), jnp.where(upper, m_rows, m_other)], axis=0)
    m_a, t = call(
        exporter_kernel,
        [(rows, rank), (cols, rank)],
        me_k, m_rows, row_all, shifts, f, col_mean,
        smem=1, scratch=[pltpu.VMEM((tall, rank + cols), jnp.float32)],
    )
    (inv_a,) = inverse_piece(after(state, t), cut, steps) if cut < steps else state
    grams = rank // 2 if ni == 2 and rank % 256 == 0 else rank
    raw_a, g_a = call(raw_kernel, [(rows, rank), (grams, rank)], top, m_a, inv_a, unit_a, smem=1)

    turns = len(bits("exp"))
    for i in range(turns):
        t_got = crossed(t, "exp", "imp", i)
        if i + 1 < turns:
            t = t + t_got
    t, m_own = call(terms_kernel, [(cols, rank), (cols, rank)], t, t_got, inv_a, unit_a, w)
    m_got = swap(m_own, "wk", 1)
    for i in range(turns):
        g_a = g_a + crossed(g_a, "exp", "imp", i)
    g_a = gather_rows(g_a, "imp") if grams < rank else g_a

    def second(*refs):
        second_kernel(rows * ne, 1, *refs)

    v, gram_a, scale_a, unit_b, *state = call(
        second, [(rank, rank), (rank, rank), (1, rank), (1, rank)] + held, after(g_a, m_own), gram_c
    )
    for bit in bits("wk")[1:]:
        m_got, v = lax.optimization_barrier((m_got, v))
        m_own = m_own + m_got
        m_got = swap(m_own, "wk", bit)
    state = [after(v, m_own), *state]
    if ni == 2:
        t_side = swap(t, "imp", 1)
        state, fac_a = inverse_piece(state, 1, steps - 1, unit=(raw_a, scale_a))
        m_got, *state = lax.optimization_barrier((m_got, *state))
        m_b = m_own + m_got
        m_side = swap(m_b, "imp", 1)
        (inv_b,) = inverse_piece([after(state[0], m_b), *state[1:]], steps - 1, steps)

        def both(*refs):
            both_kernel(cols * ni, *refs)

        raw_b, m_mine, state, scale_b, unit_c = call(
            both,
            [(cols, rank), (1, rank), (rank, rank), (1, rank), (1, rank)],
            m_b, m_side, t, t_side, scale_a, inv_b, unit_b, gram_a,
        )
    else:
        (inv_b,), fac_a = inverse_piece(state, 1, steps, unit=(raw_a, scale_a))
        raw_b, both = call(importer_kernel, [(cols, rank), (rank + 8, rank)], m_own, m_got, scale_a, inv_b, unit_b, t)
        for bit in bits("imp")[:-1]:
            both = both + swap(both, "imp", bit)
        got = swap(both, "imp", ni // 2)
        m_mine = both[rank : rank + 1] + got[rank : rank + 1]

        def third(*refs):
            third_kernel(cols * ni, *refs)

        state, scale_b, unit_c = call(third, [(rank, rank), (1, rank), (1, rank)], both, got, gram_a)
    if paired:
        far_row = swap(m_mine, "wk", 3)
        near_row = near_weeks(m_mine)
    else:
        m_all = [m_mine] + [swap(m_mine, "wk", d) for d in range(1, weeks)]
    state = inverse_piece([state], 0, steps // 2)
    if paired:
        near_row, far_row, state = lax.optimization_barrier((near_row, far_row, state))
        side_row = swap(near_row, "imp", 1)
        low = lax.axis_index("imp") == 0
        m_all = [m_mine, jnp.where(low, near_row, side_row), jnp.where(low, side_row, near_row), far_row]
    (inv_c,), fac_b = inverse_piece(state, steps // 2, steps, unit=(raw_b, scale_b))
    scratch = [pltpu.VMEM((-(-weeks // 8) * 8, rank), jnp.float32)]
    fac_c = call(week_kernel, (1, rank), *m_all, scale_a, scale_b, inv_c, unit_c, scratch=scratch)
    return (fac_a, fac_b, fac_c)


def solution(mesh):
    in_specs = (P("wk", "exp", "imp"), P("imp", None), P("wk", None))
    out_specs = (P("exp", None), P("imp", None), P("wk", None))

    return jax.shard_map(per_device, mesh=mesh, in_specs=in_specs, out_specs=out_specs, check_vma=False)
```
